32 devices in a mesh: req: 8 (over z, y), tp: 4 (over x, core).
Axes of the slice: x: 2, y: 2, z: 4, core: 2. Of those that a mesh axis runs over, the one named last changes fastest.
Arguments:
- tokens: bfloat16 [4096, 1536], P(('req', 'tp')), may hold values from -8 to 8
- attention_norm_gain: bfloat16 [1536], replicated, may hold values from 0.5 to 1.5
- expert_norm_gain: bfloat16 [1536], replicated, may hold values from 0.5 to 1.5
- query_projection: bfloat16 [1536, 1536], P(None, 'tp'), may hold values from -1 to 1
- key_projection: bfloat16 [1536, 512], P(None, 'tp'), may hold values from -1 to 1
- value_projection: bfloat16 [1536, 512], P(None, 'tp'), may hold values from -0.15625 to 0.15625
- attention_output_weight: bfloat16 [1536, 1536], P('tp'), may hold values from -0.15625 to 0.15625
- cached_keys: bfloat16 [32768, 512], P('req', 'tp'), may hold values from -6 to 6
- cached_values: bfloat16 [32768, 512], P('req', 'tp'), may hold values from -6 to 6
- token_request: int32 [8, 512], P('req'), may hold values from 0 to 3, never falling along the last dimension, each value on 1 to 256 neighbouring positions
- cached_request: int32 [8, 4096], P('req'), may hold values from 0 to 3, never falling along the last dimension, each value on 1 to 2048 neighbouring positions
- adapter_of_request: int32 [8, 4], P('req'), may hold values from 0 to 63
- adapter_table_row: int32 [64], replicated, may hold values from 0 to 63, each once
- adapter_down_maps: bfloat16 [64, 16, 1536], P('req'), may hold values from -0.15625 to 0.15625
- adapter_query_up: bfloat16 [64, 16, 1536], P('req', None, 'tp'), may hold values from -1.5 to 1.5
- adapter_value_up: bfloat16 [64, 16, 512], P('req', None, 'tp'), may hold values from -1.5 to 1.5
- routes: int32 [4096, 8], P('req'), may hold values from 0 to 31, all different within a row; in each aligned block of 128 rows (0 to 127, 128 to 255, ...) at most 34 rows name the same one
- routed_weight: float32 [4096, 8], P('req'), may hold values from 0.03 to 0.3
- expert_gate_weight: bfloat16 [32, 1536, 512], P('req', None, 'tp'), may hold values from -0.15625 to 0.15625
- expert_up_weight: bfloat16 [32, 1536, 512], P('req', None, 'tp'), may hold values from -0.15625 to 0.15625
- expert_down_weight: bfloat16 [32, 512, 1536], P('req', 'tp'), may hold values from -0.25 to 0.25
Outputs:
- mixed: bfloat16 [4096, 1536], P(('req', 'tp'))
The draws below stay inside these ranges and needn't reach their ends.
Inputs may be any that keep to these rules, and one draw needn't show every extreme that they name: `routes`: each row names 8 different experts; within each aligned block of 128 rows (the rows of one device) no expert is named by more than 34 rows, a bound that some block reaches. `token_request`: along each row the request numbers never fall; every request has 1 to 256 new tokens and one has exactly that many. `cached_request`: along each row the request numbers never fall; every request has 1 to 2048 cached tokens and one has exactly that many. `adapter_table_row`: each row number of the adapter tables appears once.
All inputs are finite; a program needn't handle non-finite values.
Results may differ from the reference program's by a relative error of at most 0.01.
Values may be sent and summed in bfloat16 or wider, within the bound.
A program may use at most 128 MiB of HBM per device.

```python
import math
import jax
import jax.numpy as jnp
import numpy as np
from jax import lax

MODEL_WIDTH = 1536
QUERY_HEADS = 24
KEY_VALUE_HEADS = 8
HEAD_SIZE = 64
EXPERTS = 32
FF_E = 512
TOP = 8
ADAPTER_RANK = 16
ADAPTER_COUNT = 64
GROUP_REQUESTS = 4
REQUEST_TOKENS = 512
CONTEXT_TOKENS = 4096
TOK_DEV = 128
TOKEN_TOTAL = 4096
EXP_CAP = 34
N_REQ = 8
N_TP = 4


def draw_tokens(key, part):
    noise = jax.random.normal(jax.random.fold_in(key, 1), (TOKEN_TOTAL, MODEL_WIDTH), jnp.float32)
    values = noise
    return jnp.clip(values, -8.0, 8.0).astype(jnp.bfloat16)


def draw_query_projection(key, part):
    drawn_weight = jax.random.normal(jax.random.fold_in(key, 3), (MODEL_WIDTH, QUERY_HEADS * HEAD_SIZE), jnp.float32) * MODEL_WIDTH ** (-0.5)
    return jnp.clip(drawn_weight, -1.0, 1.0).astype(jnp.bfloat16)


def draw_key_projection(key, part):
    drawn_weight = jax.random.normal(jax.random.fold_in(key, 4), (MODEL_WIDTH, KEY_VALUE_HEADS * HEAD_SIZE), jnp.float32) * MODEL_WIDTH ** (-0.5)
    return jnp.clip(drawn_weight, -1.0, 1.0).astype(jnp.bfloat16)


def plant(entries, rng, low, top_value):
    place = [jax.random.randint(jax.random.fold_in(rng, axis), (), 0, length) for axis, length in enumerate(entries.shape)]
    widest = entries.shape.index(max(entries.shape))
    beside = place[:widest] + [(place[widest] + 1) % entries.shape[widest]] + place[widest + 1:]
    return entries.at[tuple(place)].set(low).at[tuple(beside)].set(top_value)


def shard_levels(rng, shape, cuts, least, top_value):
    factor_of, own = 1.0, jax.random.fold_in(rng, 6)
    for dim, parts in cuts:
        steps = jnp.exp(jax.random.uniform(jax.random.fold_in(own, dim), (parts,), jnp.float32, least / len(cuts), top_value / len(cuts)))
        factor_of = factor_of * jnp.repeat(steps, shape[dim] // parts).reshape([-1 if axis == dim else 1 for axis in range(len(shape))])
    return factor_of


def length_profile(count, total, bound, skew):
    weights = [(1 << 20) // math.isqrt(standing ** skew) + 1 for standing in range(2, count + 1)]
    spare, given = total - bound - (count - 1), [1] * (count - 1)
    while spare > 0:
        movable = [i for i in range(count - 1) if given[i] < bound]
        pool, left = sum([weights[i] for i in movable]), spare
        for i in movable:
            more = min(bound - given[i], max(1, left * weights[i] // pool), spare)
            given[i] = given[i] + more
            spare = spare - more
    return np.array([bound] + given)


def ragged(own_key, count, total, bound, skew):
    if count == 2:
        one = jax.random.randint(own_key, (), max(1, total - bound), min(bound, total - 1) + 1)
        return jnp.stack([one, total - one])
    lengths = jnp.asarray(length_profile(count, total, bound, skew), jnp.int32)
    couples = (count - 1) // 2
    source_of, taker = lengths[1:1 + 2 * couples:2], lengths[2:2 + 2 * couples:2]
    room = jnp.minimum(source_of - 1, bound - taker)
    passed = jax.random.randint(jax.random.fold_in(own_key, 1), (couples,), 0, 1 << 20) % (room + 1)
    lengths = lengths.at[1:1 + 2 * couples:2].set(source_of - passed).at[2:2 + 2 * couples:2].set(taker + passed)
    return lengths[jax.random.permutation(jax.random.fold_in(own_key, 2), count)]


def deal_out(own_key, own, number, rows, number_of, top, most, lean):
    order = jax.random.permutation(own_key, number_of)
    crowded, usual = shares(number_of, rows * top, most, lean, True), shares(number_of, rows * top, most, lean, False)
    places = jnp.arange(number_of)

    def named(sizes, offset_by):
        used = int((sizes > 0).sum())
        fixed = max(1, used // 4)
        moved = fixed + (places - fixed + offset_by * (used - fixed)) % max(1, number_of - fixed)
        return jnp.zeros((number_of,), jnp.int32).at[order[jnp.where(places < fixed, places, moved)]].set(jnp.asarray(sizes, jnp.int32))

    sizes = jnp.where(number % 4 == 0, named(crowded, number // 4), named(usual, number - number // 4 - 1))
    mixed = jax.random.permutation(jax.random.fold_in(own, 3), number_of)
    source_of, taker = mixed[0:number_of // 2 * 2:2], mixed[1:number_of // 2 * 2:2]
    slack = jnp.minimum(sizes[source_of] - 1, most - sizes[taker]) // 2
    slack = jnp.where((source_of == order[0]) | (taker == order[0]) | (sizes[taker] == 0), 0, jnp.maximum(slack, 0))
    moved = jax.random.randint(jax.random.fold_in(own, 4), (number_of // 2,), 0, 1 << 20) % (slack + 1)
    sizes = sizes.at[source_of].add(-moved).at[taker].add(moved)
    items = jnp.searchsorted(jnp.cumsum(sizes), jnp.arange(rows * top), side="right").astype(jnp.int32)
    listing = items.reshape(top, rows).T
    listing = listing[jax.random.permutation(jax.random.fold_in(own, 1), rows)]
    offset_by = jax.random.randint(jax.random.fold_in(own, 2), (rows, 1), 0, top)
    return jnp.take_along_axis(listing, (jnp.arange(top)[None, :] + offset_by) % top, axis=1)


def shares(amount, total, reach, lean, full):
    portions = [(1 << 20) // math.isqrt(standing ** lean) + 1 for standing in range(1, amount + 1)]
    largest = reach if full else min(reach, max(-(-total // amount), total * portions[0] // sum(portions)))
    least = 1 if total - largest >= amount - 1 else 0
    given, rest = [largest] + [least] * (amount - 1), total - largest - least * (amount - 1)
    while rest > 0:
        free = [i for i in range(1, amount) if given[i] < largest] or [i for i in range(1, amount) if given[i] < reach]
        whole, left = sum([portions[i] for i in free]), rest
        for i in free:
            addition = min(reach - given[i], max(1, left * portions[i] // whole), rest)
            given[i] = given[i] + addition
            rest = rest - addition
    return np.array(given)


def normal_values(key, shape, width, limit, cuts=(), kind=jnp.bfloat16):
    values = width * jax.random.normal(key, shape, jnp.float32)
    if cuts:
        values = values * shard_levels(key, shape, cuts, -0.22, 0.18)
    return jnp.clip(values, -limit, limit).astype(kind)


def setup_inputs(seed: int = 0) -> dict:
    arg_keys = jax.random.split(jax.random.key(seed), 22)
    tokens = draw_tokens(jax.random.fold_in(arg_keys[21], 71), 0)
    attention_norm_gain = jnp.clip(1.0 + 0.1 * jax.random.normal(arg_keys[1], (MODEL_WIDTH,), jnp.float32), 0.5, 1.5).astype(jnp.bfloat16)
    expert_norm_gain = jnp.clip(1.0 + 0.1 * jax.random.normal(arg_keys[2], (MODEL_WIDTH,), jnp.float32), 0.5, 1.5).astype(jnp.bfloat16)
    query_projection = draw_query_projection(jax.random.fold_in(arg_keys[21], 71), 0)
    key_projection = draw_key_projection(jax.random.fold_in(arg_keys[21], 71), 0)
    value_projection = normal_values(arg_keys[5], (MODEL_WIDTH, KEY_VALUE_HEADS * HEAD_SIZE), MODEL_WIDTH ** -0.5, 0.15625, ((1, 4),))
    attention_output_weight = normal_values(arg_keys[6], (QUERY_HEADS * HEAD_SIZE, MODEL_WIDTH), (QUERY_HEADS * HEAD_SIZE) ** -0.5, 0.15625, ((0, 4),))
    cached_keys = normal_values(arg_keys[7], (N_REQ * CONTEXT_TOKENS, KEY_VALUE_HEADS * HEAD_SIZE), 1.0, 6.0, ((0, 8), (1, 4)))
    cached_values = normal_values(arg_keys[8], (N_REQ * CONTEXT_TOKENS, KEY_VALUE_HEADS * HEAD_SIZE), 1.0, 6.0, ((0, 8), (1, 4)))
    token_request = jax.vmap(lambda own: jnp.searchsorted(jnp.cumsum(ragged(own, GROUP_REQUESTS, REQUEST_TOKENS, REQUEST_TOKENS // 2, 2)), jnp.arange(REQUEST_TOKENS), side="right"))(jax.random.split(arg_keys[9], N_REQ)).reshape((N_REQ, REQUEST_TOKENS)).astype(jnp.int32)
    cached_request = jax.vmap(lambda own: jnp.searchsorted(jnp.cumsum(ragged(own, GROUP_REQUESTS, CONTEXT_TOKENS, CONTEXT_TOKENS // 2, 2)), jnp.arange(CONTEXT_TOKENS), side="right"))(jax.random.split(arg_keys[10], N_REQ)).reshape((N_REQ, CONTEXT_TOKENS)).astype(jnp.int32)
    adapter_of_request = plant(jax.random.randint(arg_keys[11], (N_REQ, GROUP_REQUESTS), 0, ADAPTER_COUNT), jax.random.fold_in(arg_keys[11], 1), 0, ADAPTER_COUNT - 1).astype(jnp.int32)
    adapter_table_row = jax.random.permutation(arg_keys[12], ADAPTER_COUNT).astype(jnp.int32)
    adapter_down_maps = normal_values(arg_keys[13], (ADAPTER_COUNT, ADAPTER_RANK, MODEL_WIDTH), MODEL_WIDTH ** -0.5, 0.15625, ((0, 8),))
    adapter_query_up = normal_values(arg_keys[14], (ADAPTER_COUNT, ADAPTER_RANK, QUERY_HEADS * HEAD_SIZE), ADAPTER_RANK ** -0.5, 1.5, ((0, 8), (2, 4)))
    adapter_value_up = normal_values(arg_keys[15], (ADAPTER_COUNT, ADAPTER_RANK, KEY_VALUE_HEADS * HEAD_SIZE), ADAPTER_RANK ** -0.5, 1.5, ((0, 8), (2, 4)))
    routes_keys = jax.random.split(jax.random.fold_in(arg_keys[16], 1), TOKEN_TOTAL // TOK_DEV)
    routes_turns = jax.random.permutation(jax.random.fold_in(arg_keys[16], 3), TOKEN_TOTAL // TOK_DEV)
    routes = jax.vmap(lambda own, number: deal_out(jax.random.fold_in(arg_keys[16], 2), own, number, TOK_DEV, EXPERTS, TOP, EXP_CAP, 0))(routes_keys, routes_turns).reshape((TOKEN_TOTAL, TOP))
    routed_weight = jnp.clip(jnp.exp(math.log(0.3) - 2.3025852 * jax.random.uniform(arg_keys[17], (TOKEN_TOTAL, TOP), jnp.float32) ** shard_levels(arg_keys[17], (TOKEN_TOTAL, TOP), ((0, 8),), -0.2, 0.2)), 0.03, 0.3)
    expert_gate_weight = normal_values(arg_keys[18], (EXPERTS, MODEL_WIDTH, FF_E), MODEL_WIDTH ** -0.5, 0.15625, ((0, 8), (2, 4)))
    expert_up_weight = normal_values(arg_keys[19], (EXPERTS, MODEL_WIDTH, FF_E), MODEL_WIDTH ** -0.5, 0.15625, ((0, 8), (2, 4)))
    expert_down_weight = normal_values(arg_keys[20], (EXPERTS, FF_E, MODEL_WIDTH), FF_E ** -0.5, 0.25, ((0, 8), (1, 4)))
    return {"tokens": tokens, "attention_norm_gain": attention_norm_gain, "expert_norm_gain": expert_norm_gain, "query_projection": query_projection, "key_projection": key_projection, "value_projection": value_projection, "attention_output_weight": attention_output_weight, "cached_keys": cached_keys, "cached_values": cached_values, "token_request": token_request, "cached_request": cached_request, "adapter_of_request": adapter_of_request, "adapter_table_row": adapter_table_row, "adapter_down_maps": adapter_down_maps, "adapter_query_up": adapter_query_up, "adapter_value_up": adapter_value_up, "routes": routes, "routed_weight": routed_weight, "expert_gate_weight": expert_gate_weight, "expert_up_weight": expert_up_weight, "expert_down_weight": expert_down_weight}


norm_eps = 1e-05
rope_theta = 10000.0

def rms_norm(row_block, gain_row):
    values = row_block.astype(jnp.float32)
    inv_rms = lax.rsqrt(lax.optimization_barrier(jnp.mean(values * values, axis=-1, keepdims=True)) + norm_eps)
    return (values * inv_rms * gain_row.astype(jnp.float32)).astype(jnp.bfloat16)

def apply_rotation(vectors, token_places, head_count):
    row_count = vectors.shape[0]
    head_width = vectors.shape[1] // head_count
    half_width = head_width // 2
    shaped = vectors.reshape(row_count, head_count, head_width)
    spacing = jnp.arange(half_width).astype(jnp.float32) / half_width
    inverse_freq = rope_theta ** (-spacing)
    angles = token_places.astype(jnp.float32)[:, None] * inverse_freq[None, :]
    cosine = jnp.cos(angles)[:, None, :]
    sine_part = jnp.sin(angles)[:, None, :]
    front = shaped[:, :, :half_width]
    behind = shaped[:, :, half_width:]
    turned = jnp.concatenate([front * cosine - behind * sine_part, behind * cosine + front * sine_part], axis=2)
    return turned.reshape(row_count, head_count * head_width)

def token_positions(new_labels, old_labels, requests):
    labels = jnp.arange(requests, dtype=jnp.int32)
    member = (new_labels[:, None] == labels[None, :]).astype(jnp.int32)
    cached = lax.optimization_barrier(jnp.sum((old_labels[:, None] == labels[None, :]).astype(jnp.int32), axis=0))
    seg_start = lax.optimization_barrier(jnp.sum((new_labels[:, None] < labels[None, :]).astype(jnp.int32), axis=0))
    offsets = lax.optimization_barrier(jnp.sum(member * (cached - seg_start)[None, :], axis=1))
    return jnp.arange(new_labels.shape[0], dtype=jnp.int32) + offsets

def allowed_keys(new_labels, old_labels):
    row_count = new_labels.shape[0]
    old_part = old_labels[None, :] == new_labels[:, None]
    causal = jnp.arange(row_count)[None, :] <= jnp.arange(row_count)[:, None]
    new_part = (new_labels[None, :] == new_labels[:, None]) & causal
    return jnp.concatenate([old_part, new_part], axis=1)

def attend_head(query_head, key_head, value_head, allowed):
    scores = lax.dot_general(query_head, key_head, (((1,), (1,)), ((), ())), preferred_element_type=jnp.float32)
    scores = jnp.where(allowed, scores * query_head.shape[1] ** (-0.5), -jnp.inf)
    row_max = lax.optimization_barrier(jnp.max(scores, axis=1, keepdims=True))
    weights = jnp.exp(scores - row_max)
    row_total = lax.optimization_barrier(jnp.sum(weights, axis=1, keepdims=True))
    mixed_rows = jnp.dot(weights.astype(jnp.bfloat16), value_head, preferred_element_type=jnp.float32)
    return (mixed_rows / row_total).astype(jnp.bfloat16)

def slot_table(route_block, expert_count, capacity):
    flat_routes = route_block.reshape(-1)
    member = (flat_routes[:, None] == jnp.arange(expert_count, dtype=jnp.int32)[None, :]).astype(jnp.int32)
    before = jnp.cumsum(member, axis=0) - member
    slot_in = lax.optimization_barrier(jnp.sum(before * member, axis=1))
    slot_index = flat_routes * capacity + slot_in
    token_ids = jnp.arange(flat_routes.shape[0], dtype=jnp.int32) // route_block.shape[1]
    holders = jnp.full((expert_count * capacity,), -1, jnp.int32).at[slot_index].set(token_ids)
    return (slot_index, holders)

def reference(tokens, attention_norm_gain, expert_norm_gain, query_projection, key_projection, value_projection, attention_output_weight, cached_keys, cached_values, token_request, cached_request, adapter_of_request, adapter_table_row, adapter_down_maps, adapter_query_up, adapter_value_up, routes, routed_weight, expert_gate_weight, expert_up_weight, expert_down_weight):
    group_results = QUERY_HEADS // KEY_VALUE_HEADS

    def layer_for_group(group_items):
        group_rows, new_labels, old_labels, adapters, old_keys, old_values = group_items
        normed = rms_norm(group_rows, attention_norm_gain)
        table_rows = adapter_table_row[adapters]
        member = (new_labels[:, None] == jnp.arange(GROUP_REQUESTS, dtype=jnp.int32)[None, :]).astype(jnp.float32)
        spread = jnp.repeat(member, ADAPTER_RANK, axis=1)
        down_selected = adapter_down_maps[table_rows].reshape(GROUP_REQUESTS * ADAPTER_RANK, MODEL_WIDTH)
        low_codes = lax.dot_general(normed, down_selected, (((1,), (1,)), ((), ())), preferred_element_type=jnp.float32)
        low_codes = (low_codes * spread).astype(jnp.bfloat16)
        query_up_selected = adapter_query_up[table_rows].reshape(GROUP_REQUESTS * ADAPTER_RANK, QUERY_HEADS * HEAD_SIZE)
        value_up_selected = adapter_value_up[table_rows].reshape(GROUP_REQUESTS * ADAPTER_RANK, KEY_VALUE_HEADS * HEAD_SIZE)
        query_rows = jnp.dot(normed, query_projection, preferred_element_type=jnp.float32) + jnp.dot(low_codes, query_up_selected, preferred_element_type=jnp.float32)
        fresh_keys = jnp.dot(normed, key_projection, preferred_element_type=jnp.float32)
        value_new = (jnp.dot(normed, value_projection, preferred_element_type=jnp.float32) + jnp.dot(low_codes, value_up_selected, preferred_element_type=jnp.float32)).astype(jnp.bfloat16)
        token_places = token_positions(new_labels, old_labels, GROUP_REQUESTS)
        query_rows = apply_rotation(query_rows, token_places, QUERY_HEADS).astype(jnp.bfloat16)
        fresh_keys = apply_rotation(fresh_keys, token_places, KEY_VALUE_HEADS).astype(jnp.bfloat16)
        key_rows = jnp.concatenate([old_keys, fresh_keys], axis=0)
        value_rows = jnp.concatenate([old_values, value_new], axis=0)
        allowed = allowed_keys(new_labels, old_labels)

        def one_head(head_id):
            query_head = lax.dynamic_slice_in_dim(query_rows, head_id * HEAD_SIZE, HEAD_SIZE, 1)
            key_head = lax.dynamic_slice_in_dim(key_rows, head_id // group_results * HEAD_SIZE, HEAD_SIZE, 1)
            value_head = lax.dynamic_slice_in_dim(value_rows, head_id // group_results * HEAD_SIZE, HEAD_SIZE, 1)
            return attend_head(query_head, key_head, value_head, allowed)
        attended = lax.map(one_head, jnp.arange(QUERY_HEADS, dtype=jnp.int32))
        attended = jnp.transpose(attended, (1, 0, 2)).reshape(REQUEST_TOKENS, QUERY_HEADS * HEAD_SIZE)
        attn_out = jnp.dot(attended, attention_output_weight, preferred_element_type=jnp.float32)
        return (group_rows.astype(jnp.float32) + attn_out).astype(jnp.bfloat16)
    residual_stream = lax.map(layer_for_group, (tokens.reshape(N_REQ, REQUEST_TOKENS, MODEL_WIDTH), token_request, cached_request, adapter_of_request, cached_keys.reshape(N_REQ, CONTEXT_TOKENS, KEY_VALUE_HEADS * HEAD_SIZE), cached_values.reshape(N_REQ, CONTEXT_TOKENS, KEY_VALUE_HEADS * HEAD_SIZE))).reshape(TOKEN_TOTAL, MODEL_WIDTH)
    ffn_rows = rms_norm(residual_stream, expert_norm_gain)
    block_count = TOKEN_TOTAL // TOK_DEV
    slot_index, holders = jax.vmap(lambda route_block: slot_table(route_block, EXPERTS, EXP_CAP))(routes.reshape(block_count, TOK_DEV, TOP))
    block_base = (jnp.arange(block_count, dtype=jnp.int32) * TOK_DEV)[:, None]
    holders = jnp.where(holders >= 0, holders + block_base, -1)
    slot_gate = jax.vmap(lambda where_to, gate_rows: jnp.zeros((EXPERTS * EXP_CAP,), jnp.float32).at[where_to].set(gate_rows.reshape(-1)))(slot_index, routed_weight.reshape(block_count, TOK_DEV * TOP))
    holders = jnp.transpose(holders.reshape(block_count, EXPERTS, EXP_CAP), (1, 0, 2)).reshape(EXPERTS, block_count * EXP_CAP)
    slot_gate = jnp.transpose(slot_gate.reshape(block_count, EXPERTS, EXP_CAP), (1, 0, 2)).reshape(EXPERTS, block_count * EXP_CAP)
    quarter = FF_E // N_TP

    def add_expert(moe_total, expert_items):
        holder_row, gate_row, gate_weight, up_weight, down_weight = expert_items
        filled = holder_row >= 0
        picked = jnp.take(ffn_rows, jnp.maximum(holder_row, 0), axis=0)
        picked = jnp.where(filled[:, None], picked, jnp.zeros_like(picked))
        gate_part = jnp.dot(picked, gate_weight, preferred_element_type=jnp.float32)
        up_part = jnp.dot(picked, up_weight, preferred_element_type=jnp.float32)
        hidden = (jax.nn.silu(gate_part) * up_part).astype(jnp.bfloat16)
        pieces = hidden.reshape(-1, N_TP, quarter).astype(jnp.float32)
        down_parts = down_weight.reshape(N_TP, quarter, MODEL_WIDTH).astype(jnp.float32)
        partial_value = jnp.einsum('rqf,qfd->qrd', pieces, down_parts)
        expert_rows = lax.optimization_barrier(jnp.sum(partial_value.astype(jnp.bfloat16).astype(jnp.float32), axis=0))
        weighted = jnp.where(filled[:, None], gate_row[:, None] * expert_rows, jnp.zeros_like(expert_rows))
        return (moe_total.at[jnp.maximum(holder_row, 0)].add(weighted), None)
    moe_start = jnp.zeros((TOKEN_TOTAL, MODEL_WIDTH), jnp.float32)
    moe_total = lax.scan(add_expert, moe_start, (holders, slot_gate, expert_gate_weight, expert_up_weight, expert_down_weight))[0]
    return (residual_stream.astype(jnp.float32) + moe_total).astype(jnp.bfloat16)
```

```python
import functools

import jax
import jax.numpy as jnp
from jax import lax
from jax.experimental import pallas as pl
from jax.experimental.pallas import tpu as pltpu
from jax.sharding import PartitionSpec as P

HEAD_SIZE = 64
EXPERTS = 32
TOP = 8
ADAPTER_RANK = 16
GROUP_REQUESTS = 4
LANES = 128
KEY_BLOCK = 512
QUERY_BLOCK = 128
HIDDEN_SCORE = -1e30

norm_eps = 1e-05
rope_theta = 10000.0


def rms_norm(row_block, gain_row):
    values = row_block.astype(jnp.float32)
    inv_rms = lax.rsqrt(jnp.mean(values * values, axis=-1, keepdims=True) + norm_eps)
    return (values * inv_rms * gain_row.astype(jnp.float32)).astype(jnp.bfloat16)


def dot_f32(left, right):
    return jnp.dot(left, right, preferred_element_type=jnp.float32)


def projection_kernel(
    heads, kv_heads, x_ref, gain_ref, wq_ref, wk_ref, wv_ref, down_ref, qup_ref, vup_ref,
    spread_ref, cos_ref, sin_ref, q_ref, k_ref, v_ref
):
    normed = rms_norm(x_ref[...], gain_ref[...])
    low = lax.dot_general(
        normed, down_ref[...], (((1,), (1,)), ((), ())), preferred_element_type=jnp.float32
    )
    low = (low * spread_ref[...]).astype(jnp.bfloat16)
    q = dot_f32(normed, wq_ref[...]) + dot_f32(low, qup_ref[...])
    k = dot_f32(normed, wk_ref[...])
    v_ref[...] = (dot_f32(normed, wv_ref[...]) + dot_f32(low, vup_ref[...])).astype(jnp.bfloat16)
    cosine, sine = cos_ref[...], sin_ref[...]
    lane = lax.broadcasted_iota(jnp.int32, cosine.shape, 1)
    front = lane % HEAD_SIZE < HEAD_SIZE // 2
    upper = lane >= HEAD_SIZE

    def turn(piece):
        partner = jnp.where(
            front,
            pltpu.roll(piece, LANES - HEAD_SIZE // 2, 1),
            pltpu.roll(piece, HEAD_SIZE // 2, 1),
        )
        return piece * cosine + partner * sine

    k_ref[...] = turn(k).astype(jnp.bfloat16)
    per_kv = heads // kv_heads
    for piece_id in range(heads // 2):
        turned = turn(q[:, piece_id * LANES : (piece_id + 1) * LANES]) * HEAD_SIZE ** (-0.5)
        swapped = pltpu.roll(turned, HEAD_SIZE, 1)
        for side in range(2):
            head = 2 * piece_id + side
            kv = head // per_kv
            source = turned if kv == side else swapped
            keep = upper if kv == 1 else jnp.logical_not(upper)
            q_ref[head] = jnp.where(keep, source, 0.0).astype(jnp.bfloat16)


def attention_kernel(
    heads, kv_heads, range_ref, q_ref, ck_ref, cv_ref, nk_ref, nv_ref, bound_ref, wo_ref, out_ref
):
    block = pl.program_id(0)
    rows = q_ref.shape[1]
    queries = q_ref[...].reshape(heads * rows, LANES)
    bounds = jnp.concatenate([bound_ref[...]] * heads, axis=1)
    old_start, old_end, new_start, new_end = (bounds[i : i + 1] for i in range(4))

    def score(keys, first, start, end):
        values = lax.dot_general(
            keys, queries, (((1,), (1,)), ((), ())), preferred_element_type=jnp.float32
        )
        place = lax.broadcasted_iota(jnp.int32, values.shape, 0) + first
        return jnp.where((place >= start) & (place < end), values, HIDDEN_SCORE)

    def gather(weights, values):
        return lax.dot_general(
            values, weights.astype(jnp.bfloat16), (((0,), (0,)), ((), ())),
            preferred_element_type=jnp.float32,
        )

    scores = score(nk_ref[...], 0, new_start, new_end)
    top = jnp.max(scores, axis=0, keepdims=True)
    weights = jnp.exp(scores - top)
    total = jnp.sum(weights, axis=0, keepdims=True)
    mixed = gather(weights, nv_ref[...])

    def step(index, carry):
        top, total, mixed = carry
        first = pl.multiple_of(index * KEY_BLOCK, KEY_BLOCK)
        scores = score(ck_ref[pl.ds(first, KEY_BLOCK), :], first, old_start, old_end)
        new_top = jnp.maximum(top, jnp.max(scores, axis=0, keepdims=True))
        shrink = jnp.exp(top - new_top)
        weights = jnp.exp(scores - new_top)
        total = total * shrink + jnp.sum(weights, axis=0, keepdims=True)
        mixed = mixed * shrink + gather(weights, cv_ref[pl.ds(first, KEY_BLOCK), :])
        return new_top, total, mixed

    top, total, mixed = lax.fori_loop(
        range_ref[0, block], range_ref[1, block], step, (top, total, mixed)
    )
    mixed = mixed / total
    per_kv = heads // kv_heads
    pieces = []
    for piece_id in range(heads // 2):
        halves = []
        for head in (2 * piece_id, 2 * piece_id + 1):
            kv = head // per_kv
            halves.append(
                mixed[kv * HEAD_SIZE : (kv + 1) * HEAD_SIZE, head * rows : (head + 1) * rows]
            )
        pieces.append(jnp.transpose(jnp.concatenate(halves, axis=0)).astype(jnp.bfloat16))
    out_ref[...] = dot_f32(jnp.concatenate(pieces, axis=1), wo_ref[...]).astype(jnp.bfloat16)


def expert_kernel(slots, x_ref, slot_ref, weight_ref, *refs):
    gates, ups, downs = refs[0:4], refs[4:8], refs[8:12]
    out_ref, total_ref = refs[12:]
    expert = pl.program_id(1)
    rows = x_ref.shape[0]
    chosen = lax.broadcasted_iota(jnp.int32, (slots, rows), 0) == slot_ref[0]
    row_weight = jnp.sum(jnp.where(chosen, weight_ref[0], 0.0), axis=1, keepdims=True)
    pick = jnp.where(chosen, 1.0, 0.0).astype(jnp.bfloat16)
    picked = dot_f32(pick, x_ref[...]).astype(jnp.bfloat16)
    gate = dot_f32(picked, jnp.concatenate([ref[0] for ref in gates], axis=1))
    up = dot_f32(picked, jnp.concatenate([ref[0] for ref in ups], axis=1))
    hidden = (jax.nn.silu(gate) * up).astype(jnp.bfloat16)
    result = dot_f32(hidden, jnp.concatenate([ref[0] for ref in downs], axis=0))
    result = (result * row_weight).astype(jnp.bfloat16)
    spread = lax.dot_general(
        pick, result, (((0,), (0,)), ((), ())), preferred_element_type=jnp.float32
    )

    @pl.when(expert == 0)
    def _():
        total_ref[...] = spread

    @pl.when(expert > 0)
    def _():
        total_ref[...] += spread

    @pl.when(expert == pl.num_programs(1) - 1)
    def _():
        out_ref[...] = total_ref[...].astype(jnp.bfloat16)


def on_device(
    tokens,
    attention_norm_gain,
    expert_norm_gain,
    query_projection,
    key_projection,
    value_projection,
    attention_output_weight,
    cached_keys,
    cached_values,
    token_request,
    cached_request,
    adapter_of_request,
    adapter_table_row,
    adapter_down_maps,
    adapter_query_up,
    adapter_value_up,
    routes,
    routed_weight,
    expert_gate_weight,
    expert_up_weight,
    expert_down_weight,
):
    tp_count = lax.axis_size("tp")
    tp_place = lax.axis_index("tp")
    req_count = lax.axis_size("req")
    req_place = lax.axis_index("req")
    own_rows, width = tokens.shape
    group_size = own_rows * tp_count
    query_width = query_projection.shape[1]
    kv_width = key_projection.shape[1]
    heads = query_width // HEAD_SIZE
    kv_heads = kv_width // HEAD_SIZE
    low_rows = GROUP_REQUESTS * ADAPTER_RANK
    assert tp_count == 4 and kv_heads == 2 and own_rows == QUERY_BLOCK
    capacity = own_rows * TOP // EXPERTS + 2

    own_routes = lax.dynamic_slice_in_dim(routes, tp_place * own_rows, own_rows, 0)
    own_gates = lax.dynamic_slice_in_dim(routed_weight, tp_place * own_rows, own_rows, 0)
    wanted_row = jnp.pad(
        adapter_of_request.astype(jnp.float32),
        ((0, 7), (0, own_rows - adapter_of_request.shape[1])),
    )
    notes = jnp.concatenate([own_routes.T.astype(jnp.float32), own_gates.T, wanted_row], axis=0)
    notes = lax.all_gather(notes, "req", axis=0, tiled=False)
    all_routes = notes[:, :TOP].astype(jnp.int32)
    all_gates = notes[:, TOP : 2 * TOP]
    wanted = notes[:, 2 * TOP, :GROUP_REQUESTS].astype(jnp.int32).reshape(-1)

    group_x = lax.all_gather(tokens, "tp", axis=0, tiled=True)

    across = [(i, i ^ 2) for i in range(tp_count)]
    beside = [(i, i ^ 1) for i in range(tp_count)]

    def quarters(piece):
        far = lax.ppermute(piece, "tp", across)
        near = lax.ppermute(piece, "tp", beside)
        far_near = lax.ppermute(far, "tp", beside)
        return [piece, far, near, far_near]

    gates, ups, downs = (
        quarters(expert_gate_weight), quarters(expert_up_weight), quarters(expert_down_weight)
    )

    catalog = jnp.arange(adapter_table_row.shape[0], dtype=jnp.int32)
    table_rows = jnp.sum(
        (wanted[:, None] == catalog[None, :]).astype(jnp.int32) * adapter_table_row[None, :], axis=1
    )
    stored = adapter_down_maps.shape[0]
    local_rows = req_place * stored + jnp.arange(stored, dtype=jnp.int32)
    mine = (table_rows[:, None] == local_rows[None, :])[:, :, None, None]
    down_width = width // tp_count
    down_part = lax.dynamic_slice_in_dim(adapter_down_maps, tp_place * down_width, down_width, 2)

    def select(table):
        return jnp.sum(
            jnp.where(mine, table[None].astype(jnp.float32), 0.0), axis=1
        ).astype(jnp.bfloat16).reshape(-1, table.shape[2])

    adapters = jnp.concatenate(
        [select(down_part), select(adapter_query_up), select(adapter_value_up)], axis=1
    )
    adapters = lax.psum_scatter(adapters, "req", scatter_dimension=0, tiled=True)
    down_selected = lax.all_gather(adapters[:, :down_width], "tp", axis=1, tiled=True)
    query_up_selected = adapters[:, down_width : down_width + query_width]
    value_up_selected = adapters[:, down_width + query_width :]

    new_labels = token_request[0]
    old_labels = cached_request[0]
    labels = jnp.arange(GROUP_REQUESTS, dtype=jnp.int32)
    member = new_labels[:, None] == labels[None, :]
    old_below = jnp.sum((old_labels[:, None] < labels[None, :]).astype(jnp.int32), axis=0)
    old_upto = jnp.sum((old_labels[:, None] <= labels[None, :]).astype(jnp.int32), axis=0)
    new_below = jnp.sum((new_labels[:, None] < labels[None, :]).astype(jnp.int32), axis=0)

    def by_token(table):
        return jnp.sum(jnp.where(member, table[None, :], 0), axis=1)

    place = jnp.arange(group_size, dtype=jnp.int32)
    old_start, old_end, new_start = by_token(old_below), by_token(old_upto), by_token(new_below)
    positions = place - new_start + old_end - old_start
    bounds = jnp.stack([old_start, old_end, new_start, place + 1] * 2, axis=0)
    block_start = jnp.min(old_start.reshape(-1, QUERY_BLOCK), axis=1)
    block_end = jnp.max(old_end.reshape(-1, QUERY_BLOCK), axis=1)
    block_range = jnp.stack(
        [block_start // KEY_BLOCK, (block_end + KEY_BLOCK - 1) // KEY_BLOCK], axis=0
    )
    spread = jnp.repeat(member.astype(jnp.float32), ADAPTER_RANK, axis=1)
    half = HEAD_SIZE // 2
    lane = jnp.arange(LANES, dtype=jnp.int32)
    inverse_freq = rope_theta ** (-((lane % half).astype(jnp.float32) / half))
    angles = positions.astype(jnp.float32)[:, None] * inverse_freq[None, :]
    cosine = jnp.cos(angles)
    sine = jnp.sin(angles) * jnp.where(lane % HEAD_SIZE < half, -1.0, 1.0)[None, :]

    whole = lambda shape: pl.BlockSpec(shape, lambda i, *_: (0,) * len(shape))
    by_row = lambda rows, columns: pl.BlockSpec((rows, columns), lambda i, *_: (i, 0))
    rows = 2 * QUERY_BLOCK
    queries, fresh_keys, fresh_values = pl.pallas_call(
        functools.partial(projection_kernel, heads, kv_heads),
        grid=(group_size // rows,),
        in_specs=[
            by_row(rows, width), whole((1, width)), whole((width, query_width)),
            whole((width, kv_width)), whole((width, kv_width)), whole((low_rows, width)),
            whole((low_rows, query_width)), whole((low_rows, kv_width)), by_row(rows, low_rows),
            by_row(rows, LANES), by_row(rows, LANES),
        ],
        out_specs=[
            pl.BlockSpec((heads, rows, LANES), lambda i: (0, i, 0)),
            by_row(rows, kv_width), by_row(rows, kv_width),
        ],
        out_shape=[
            jax.ShapeDtypeStruct((heads, group_size, LANES), jnp.bfloat16),
            jax.ShapeDtypeStruct((group_size, kv_width), jnp.bfloat16),
            jax.ShapeDtypeStruct((group_size, kv_width), jnp.bfloat16),
        ],
        cost_estimate=pl.CostEstimate(
            flops=2 * group_size * width * (query_width + 2 * kv_width + low_rows),
            bytes_accessed=6_000_000, transcendentals=0,
        ),
        name="projections",
    )(
        group_x, attention_norm_gain[None, :], query_projection, key_projection, value_projection,
        down_selected, query_up_selected, value_up_selected, spread, cosine, sine,
    )

    context = cached_keys.shape[0]
    partial_rows = pl.pallas_call(
        functools.partial(attention_kernel, heads, kv_heads),
        grid_spec=pltpu.PrefetchScalarGridSpec(
            num_scalar_prefetch=1,
            grid=(group_size // QUERY_BLOCK,),
            in_specs=[
                pl.BlockSpec((heads, QUERY_BLOCK, LANES), lambda i, *_: (0, i, 0)),
                whole((context, kv_width)), whole((context, kv_width)),
                whole((group_size, kv_width)), whole((group_size, kv_width)),
                pl.BlockSpec((8, QUERY_BLOCK), lambda i, *_: (0, i)),
                whole((query_width, width)),
            ],
            out_specs=by_row(QUERY_BLOCK, width),
        ),
        out_shape=jax.ShapeDtypeStruct((group_size, width), jnp.bfloat16),
        compiler_params=pltpu.CompilerParams(vmem_limit_bytes=40 << 20),
        cost_estimate=pl.CostEstimate(
            flops=10_000_000_000, bytes_accessed=6_000_000, transcendentals=14_000_000
        ),
        name="attention",
    )(
        block_range, queries, cached_keys, cached_values, fresh_keys, fresh_values, bounds,
        attention_output_weight,
    )
    attn_own = lax.psum_scatter(partial_rows, "tp", scatter_dimension=0, tiled=True)
    resid_own = (tokens.astype(jnp.float32) + attn_own.astype(jnp.float32)).astype(jnp.bfloat16)
    ffn_own = rms_norm(resid_own, expert_norm_gain)
    arrived = lax.all_gather(ffn_own, "req", axis=0, tiled=True)

    local_experts = expert_gate_weight.shape[0]
    total_rows = req_count * own_rows
    chunk_rows = min(8, req_count) * own_rows
    chunk_blocks = chunk_rows // own_rows
    slots = chunk_blocks * capacity
    expert_ids = req_place * local_experts + jnp.arange(local_experts, dtype=jnp.int32)
    hits = all_routes[None] == expert_ids[:, None, None, None]
    expert_weight = jnp.sum(jnp.where(hits, all_gates[None], 0.0), axis=2)
    named = jnp.any(hits, axis=2)
    earlier = jnp.arange(own_rows)[:, None] < jnp.arange(own_rows)[None, :]
    rank = jnp.einsum(
        "ebt,tu->ebu", named.astype(jnp.bfloat16), earlier.astype(jnp.bfloat16),
        preferred_element_type=jnp.float32,
    ).astype(jnp.int32)
    block_base = (jnp.arange(req_count, dtype=jnp.int32) % chunk_blocks) * capacity
    slot_of = jnp.where(named, rank + block_base[None, :, None], -1)
    slot_of = slot_of.reshape(local_experts, 1, total_rows)
    expert_weight = expert_weight.reshape(local_experts, 1, total_rows)

    quarter = expert_gate_weight.shape[2]
    row_spec = pl.BlockSpec((1, 1, chunk_rows), lambda c, e: (e, 0, c))
    moe = pl.pallas_call(
        functools.partial(expert_kernel, slots),
        grid=(total_rows // chunk_rows, local_experts),
        in_specs=[pl.BlockSpec((chunk_rows, width), lambda c, e: (c, 0)), row_spec, row_spec]
        + [pl.BlockSpec((1, width, quarter), lambda c, e: (e, 0, 0))] * 8
        + [pl.BlockSpec((1, quarter, width), lambda c, e: (e, 0, 0))] * 4,
        out_specs=pl.BlockSpec((chunk_rows, width), lambda c, e: (c, 0)),
        out_shape=jax.ShapeDtypeStruct((total_rows, width), jnp.bfloat16),
        scratch_shapes=[pltpu.VMEM((chunk_rows, width), jnp.float32)],
        compiler_params=pltpu.CompilerParams(vmem_limit_bytes=52 << 20),
        cost_estimate=pl.CostEstimate(
            flops=12_000_000_000, bytes_accessed=26_000_000, transcendentals=600_000
        ),
        name="experts",
    )(arrived, slot_of, expert_weight, *gates, *ups, *downs)
    moe_own = lax.psum_scatter(moe, "req", scatter_dimension=0, tiled=True)
    return (resid_own.astype(jnp.float32) + moe_own.astype(jnp.float32)).astype(jnp.bfloat16)


def solution(mesh):
    return jax.shard_map(
        on_device,
        mesh=mesh,
        in_specs=(
            P(("req", "tp"), None),
            P(),
            P(),
            P(None, "tp"),
            P(None, "tp"),
            P(None, "tp"),
            P("tp", None),
            P("req", "tp"),
            P("req", "tp"),
            P("req", None),
            P("req", None),
            P("req", None),
            P(),
            P("req", None, None),
            P("req", None, "tp"),
            P("req", None, "tp"),
            P("req", None),
            P("req", None),
            P("req", None, "tp"),
            P("req", None, "tp"),
            P("req", "tp", None),
        ),
        out_specs=P(("req", "tp"), None),
        check_vma=False,
    )
```

```python
import functools

import jax
import jax.numpy as jnp
from jax import lax
from jax.experimental import pallas as pl
from jax.experimental.pallas import tpu as pltpu
from jax.sharding import PartitionSpec as P

HEAD_SIZE = 64
EXPERTS = 32
TOP = 8
ADAPTER_RANK = 16
GROUP_REQUESTS = 4
LANES = 128
KEY_BLOCK = 512
QUERY_BLOCK = 128
HIDDEN_SCORE = -1e30

norm_eps = 1e-05
rope_theta = 10000.0


def rms_norm(row_block, gain_row):
    values = row_block.astype(jnp.float32)
    inv_rms = lax.rsqrt(jnp.mean(values * values, axis=-1, keepdims=True) + norm_eps)
    return (values * inv_rms * gain_row.astype(jnp.float32)).astype(jnp.bfloat16)


def dot_f32(left, right):
    return jnp.dot(left, right, preferred_element_type=jnp.float32)


def projection_kernel(
    heads, kv_heads, x_ref, gain_ref, wq_ref, wk_ref, wv_ref, down_ref, qup_ref, vup_ref,
    spread_ref, cos_ref, sin_ref, q_ref, k_ref, v_ref
):
    normed = rms_norm(x_ref[...], gain_ref[...])
    low = lax.dot_general(
        normed, down_ref[...], (((1,), (1,)), ((), ())), preferred_element_type=jnp.float32
    )
    low = (low * spread_ref[...]).astype(jnp.bfloat16)
    q = dot_f32(normed, wq_ref[...]) + dot_f32(low, qup_ref[...])
    k = dot_f32(normed, wk_ref[...])
    v_ref[...] = (dot_f32(normed, wv_ref[...]) + dot_f32(low, vup_ref[...])).astype(jnp.bfloat16)
    cosine, sine = cos_ref[...], sin_ref[...]
    lane = lax.broadcasted_iota(jnp.int32, cosine.shape, 1)
    front = lane % HEAD_SIZE < HEAD_SIZE // 2
    upper = lane >= HEAD_SIZE

    def turn(piece):
        partner = jnp.where(
            front,
            pltpu.roll(piece, LANES - HEAD_SIZE // 2, 1),
            pltpu.roll(piece, HEAD_SIZE // 2, 1),
        )
        return piece * cosine + partner * sine

    k_ref[...] = turn(k).astype(jnp.bfloat16)
    per_kv = heads // kv_heads
    for piece_id in range(heads // 2):
        turned = turn(q[:, piece_id * LANES : (piece_id + 1) * LANES]) * HEAD_SIZE ** (-0.5)
        swapped = pltpu.roll(turned, HEAD_SIZE, 1)
        for side in range(2):
            head = 2 * piece_id + side
            kv = head // per_kv
            source = turned if kv == side else swapped
            keep = upper if kv == 1 else jnp.logical_not(upper)
            q_ref[head] = jnp.where(keep, source, 0.0).astype(jnp.bfloat16)


def attention_kernel(
    heads, kv_heads, range_ref, q_ref, ck_ref, cv_ref, nk_ref, nv_ref, bound_ref, wo_ref, out_ref
):
    block = pl.program_id(0)
    rows = q_ref.shape[1]
    queries = q_ref[...].reshape(heads * rows, LANES)
    bounds = jnp.concatenate([bound_ref[...]] * heads, axis=1)
    old_start, old_end, new_start, new_end = (bounds[i : i + 1] for i in range(4))

    def score(keys, first, start, end):
        values = lax.dot_general(
            keys, queries, (((1,), (1,)), ((), ())), preferred_element_type=jnp.float32
        )
        place = lax.broadcasted_iota(jnp.int32, values.shape, 0) + first
        return jnp.where((place >= start) & (place < end), values, HIDDEN_SCORE)

    def gather(weights, values):
        return lax.dot_general(
            values, weights.astype(jnp.bfloat16), (((0,), (0,)), ((), ())),
            preferred_element_type=jnp.float32,
        )

    scores = score(nk_ref[...], 0, new_start, new_end)
    top = jnp.max(scores, axis=0, keepdims=True)
    weights = jnp.exp(scores - top)
    total = jnp.sum(weights, axis=0, keepdims=True)
    mixed = gather(weights, nv_ref[...])

    def step(index, carry):
        top, total, mixed = carry
        first = pl.multiple_of(index * KEY_BLOCK, KEY_BLOCK)
        scores = score(ck_ref[pl.ds(first, KEY_BLOCK), :], first, old_start, old_end)
        new_top = jnp.maximum(top, jnp.max(scores, axis=0, keepdims=True))
        shrink = jnp.exp(top - new_top)
        weights = jnp.exp(scores - new_top)
        total = total * shrink + jnp.sum(weights, axis=0, keepdims=True)
        mixed = mixed * shrink + gather(weights, cv_ref[pl.ds(first, KEY_BLOCK), :])
        return new_top, total, mixed

    top, total, mixed = lax.fori_loop(
        range_ref[0, block], range_ref[1, block], step, (top, total, mixed)
    )
    mixed = mixed / total
    per_kv = heads // kv_heads
    pieces = []
    for piece_id in range(heads // 2):
        halves = []
        for head in (2 * piece_id, 2 * piece_id + 1):
            kv = head // per_kv
            halves.append(
                mixed[kv * HEAD_SIZE : (kv + 1) * HEAD_SIZE, head * rows : (head + 1) * rows]
            )
        pieces.append(jnp.transpose(jnp.concatenate(halves, axis=0)).astype(jnp.bfloat16))
    out_ref[...] = dot_f32(jnp.concatenate(pieces, axis=1), wo_ref[...]).astype(jnp.bfloat16)


def expert_kernel(slots, x_ref, slot_ref, weight_ref, *refs):
    gates, ups, downs = refs[0:4], refs[4:8], refs[8:12]
    out_ref, total_ref = refs[12:]
    expert = pl.program_id(1)
    rows = x_ref.shape[0]
    chosen = lax.broadcasted_iota(jnp.int32, (slots, rows), 0) == slot_ref[0]
    row_weight = jnp.sum(jnp.where(chosen, weight_ref[0], 0.0), axis=1, keepdims=True)
    pick = jnp.where(chosen, 1.0, 0.0).astype(jnp.bfloat16)
    picked = dot_f32(pick, x_ref[...]).astype(jnp.bfloat16)
    gate = dot_f32(picked, jnp.concatenate([ref[0] for ref in gates], axis=1))
    up = dot_f32(picked, jnp.concatenate([ref[0] for ref in ups], axis=1))
    hidden = (jax.nn.silu(gate) * up).astype(jnp.bfloat16)
    result = dot_f32(hidden, jnp.concatenate([ref[0] for ref in downs], axis=0))
    result = (result * row_weight).astype(jnp.bfloat16)
    spread = lax.dot_general(
        pick, result, (((0,), (0,)), ((), ())), preferred_element_type=jnp.float32
    )

    @pl.when(expert == 0)
    def _():
        total_ref[...] = spread

    @pl.when(expert > 0)
    def _():
        total_ref[...] += spread

    @pl.when(expert == pl.num_programs(1) - 1)
    def _():
        out_ref[...] = total_ref[...].astype(jnp.bfloat16)


MESH = pl.DeviceIdType.MESH


def send_to(source, target, send_sem, recv_sem, axis, device):
    return pltpu.make_async_remote_copy(
        src_ref=source, dst_ref=target, send_sem=send_sem, recv_sem=recv_sem,
        device_id={axis: device}, device_id_type=MESH,
    )


def greet(peers):
    barrier = pltpu.get_barrier_semaphore()
    for axis, device in peers:
        pl.semaphore_signal(barrier, inc=1, device_id={axis: device}, device_id_type=MESH)
    pl.semaphore_wait(barrier, len(peers))


def core_partner(place):
    return place + 1 - 2 * (place % 2)


def opening_kernel(
    req_count, tp_count, stored, tokens_ref, notes_ref, table_ref,
    group_ref, all_notes_ref, down_ref, qup_ref, vup_ref,
    noted, chosen, arrived, own_down, downs,
    local_sem, x_send, x_recv, n_send, n_recv, a_send, a_recv, d_send, d_recv
):
    me, here = lax.axis_index("req"), lax.axis_index("tp")
    beside, across = core_partner(here), (here + 2) % tp_count
    greet(
        [("req", (me + step) % req_count) for step in range(1, req_count)]
        + [("tp", (here + step) % tp_count) for step in range(1, tp_count)]
    )
    note_copies = []
    for step in range(1, req_count):
        copy = send_to(notes_ref, noted.at[step], n_send.at[step], n_recv.at[step], "req",
                       (me + step) % req_count)
        copy.start()
        note_copies.append(copy)
    own_copy = pltpu.make_async_copy(tokens_ref, group_ref.at[here], local_sem)
    own_copy.start()
    to_across = send_to(tokens_ref, group_ref.at[here], x_send.at[0], x_recv.at[0], "tp", across)
    to_across.start()
    to_beside = send_to(tokens_ref, group_ref.at[here], x_send.at[1], x_recv.at[1], "tp", beside)
    to_beside.start()

    rows = GROUP_REQUESTS * ADAPTER_RANK
    depth = stored * ADAPTER_RANK
    lane = lax.broadcasted_iota(jnp.int32, (rows, depth), 1)
    row = lax.broadcasted_iota(jnp.int32, (rows, depth), 0)
    same_rank = lane % ADAPTER_RANK == row % ADAPTER_RANK
    slot = (me * stored + lane // ADAPTER_RANK).astype(jnp.float32)

    def select(notes):
        wanted = notes[2 * TOP :, :depth]
        pick = jnp.where(same_rank & (wanted == slot), 1.0, 0.0).astype(jnp.bfloat16)
        return dot_f32(pick, table_ref[...])

    total = select(notes_ref[...])
    all_notes_ref[me] = notes_ref[: 2 * TOP, :]
    adapter_copies = []
    for step in range(1, req_count):
        note_copies[step - 1].wait()
        notes = noted[step]
        source = (me + req_count - step) % req_count
        all_notes_ref[source] = notes[: 2 * TOP, :]
        chosen[step] = select(notes).astype(jnp.bfloat16)
        copy = send_to(chosen.at[step], arrived.at[step], a_send.at[step], a_recv.at[step], "req",
                       source)
        copy.start()
        adapter_copies.append(copy)
    to_across.wait()
    forward = send_to(group_ref.at[across], group_ref.at[across], x_send.at[2], x_recv.at[2], "tp",
                      beside)
    forward.start()
    for step in range(1, req_count):
        adapter_copies[step - 1].wait()
        total = total + arrived[step].astype(jnp.float32)
    total = total.astype(jnp.bfloat16)
    down_width = own_down.shape[1]
    query_width = qup_ref.shape[1]
    own_down[...] = total[:, :down_width]
    downs[here] = total[:, :down_width]
    down_copies = []
    for step in range(1, tp_count):
        copy = send_to(own_down, downs.at[here], d_send.at[step], d_recv.at[step], "tp",
                       (here + step) % tp_count)
        copy.start()
        down_copies.append(copy)
    qup_ref[...] = total[:, down_width : down_width + query_width]
    vup_ref[...] = total[:, down_width + query_width :]
    for copy in down_copies:
        copy.wait()
    down_ref[...] = jnp.concatenate([downs[i] for i in range(tp_count)], axis=1)
    own_copy.wait()
    to_beside.wait()
    forward.wait()


def middle_kernel(
    req_count, tp_count, partial_ref, tokens_ref, gain_ref, resid_ref, arrived_ref,
    pair, joined, far, ffn, local_sem, p_send, p_recv, z_send, z_recv, f_send, f_recv
):
    me, here = lax.axis_index("req"), lax.axis_index("tp")
    beside, across = core_partner(here), (here + 2) % tp_count
    partner = core_partner(me)
    line = req_count // 2
    greet(
        [("tp", beside), ("tp", across), ("req", partner)]
        + [("req", (me + 2 * step) % req_count) for step in range(1, line)]
    )
    f32 = jnp.float32
    second = send_to(partial_ref.at[(beside + 2) % tp_count], pair.at[1], p_send.at[1],
                     p_recv.at[1], "tp", beside)
    second.start()
    first = send_to(partial_ref.at[beside], pair.at[0], p_send.at[0], p_recv.at[0], "tp", beside)
    first.start()
    second.wait()
    joined[...] = (partial_ref[across].astype(f32) + pair[1].astype(f32)).astype(jnp.bfloat16)
    last = send_to(joined, far, p_send.at[2], p_recv.at[2], "tp", across)
    last.start()
    first.wait()
    own = partial_ref[here].astype(f32) + pair[0].astype(f32) + tokens_ref[...].astype(f32)
    last.wait()
    resid = (own + far[...].astype(f32)).astype(jnp.bfloat16)
    resid_ref[...] = resid
    ffn[...] = rms_norm(resid, gain_ref[...])
    line_copies = []
    for step in range(1, line):
        copy = send_to(ffn, arrived_ref.at[me], z_send.at[step], z_recv.at[step], "req",
                       (me + 2 * step) % req_count)
        copy.start()
        line_copies.append(copy)
    to_partner = send_to(ffn, arrived_ref.at[me], f_send.at[0], f_recv.at[0], "req", partner)
    to_partner.start()
    own_copy = pltpu.make_async_copy(ffn, arrived_ref.at[me], local_sem)
    own_copy.start()
    forwards = []
    for step in range(1, line):
        line_copies[step - 1].wait()
        source = (me + req_count - 2 * step) % req_count
        copy = send_to(arrived_ref.at[source], arrived_ref.at[source], f_send.at[step],
                       f_recv.at[step], "req", partner)
        copy.start()
        forwards.append(copy)
    own_copy.wait()
    to_partner.wait()
    for copy in forwards:
        copy.wait()


def closing_kernel(
    req_count, moe_ref, resid_ref, out_ref, beside_in, line_out, line_in,
    y_send, y_recv, z_send, z_recv
):
    me = lax.axis_index("req")
    partner = core_partner(me)
    line = req_count // 2
    greet(
        [("req", partner)]
        + [("req", (me + 2 * step) % req_count) for step in range(1, line)]
    )
    f32 = jnp.float32
    order = list(range(1, line)) + [0]
    beside_copies = {}
    for step in order:
        copy = send_to(moe_ref.at[(partner + 2 * step) % req_count], beside_in.at[step],
                       y_send.at[step], y_recv.at[step], "req", partner)
        copy.start()
        beside_copies[step] = copy
    line_copies = []
    for step in range(1, line):
        target = (me + 2 * step) % req_count
        beside_copies[step].wait()
        line_out[step] = (
            moe_ref[target].astype(f32) + beside_in[step].astype(f32)
        ).astype(jnp.bfloat16)
        copy = send_to(line_out.at[step], line_in.at[step], z_send.at[step], z_recv.at[step],
                       "req", target)
        copy.start()
        line_copies.append(copy)
    beside_copies[0].wait()
    total = resid_ref[...].astype(f32) + moe_ref[me].astype(f32) + beside_in[0].astype(f32)
    for step in range(1, line):
        line_copies[step - 1].wait()
        total = total + line_in[step].astype(f32)
    out_ref[...] = total.astype(jnp.bfloat16)


def on_device(
    tokens,
    attention_norm_gain,
    expert_norm_gain,
    query_projection,
    key_projection,
    value_projection,
    attention_output_weight,
    cached_keys,
    cached_values,
    token_request,
    cached_request,
    adapter_of_request,
    adapter_table_row,
    adapter_down_maps,
    adapter_query_up,
    adapter_value_up,
    routes,
    routed_weight,
    expert_gate_weight,
    expert_up_weight,
    expert_down_weight,
):
    tp_count = lax.axis_size("tp")
    tp_place = lax.axis_index("tp")
    req_count = lax.axis_size("req")
    req_place = lax.axis_index("req")
    own_rows, width = tokens.shape
    group_size = own_rows * tp_count
    query_width = query_projection.shape[1]
    kv_width = key_projection.shape[1]
    heads = query_width // HEAD_SIZE
    kv_heads = kv_width // HEAD_SIZE
    low_rows = GROUP_REQUESTS * ADAPTER_RANK
    assert tp_count == 4 and kv_heads == 2 and own_rows == QUERY_BLOCK
    capacity = own_rows * TOP // EXPERTS + 2

    own_routes = lax.dynamic_slice_in_dim(routes, tp_place * own_rows, own_rows, 0)
    own_gates = lax.dynamic_slice_in_dim(routed_weight, tp_place * own_rows, own_rows, 0)
    catalog = jnp.arange(adapter_table_row.shape[0], dtype=jnp.int32)
    table_rows = jnp.sum(
        (adapter_of_request[0][:, None] == catalog[None, :]).astype(jnp.int32)
        * adapter_table_row[None, :],
        axis=1,
    )
    wanted = jnp.broadcast_to(
        jnp.repeat(table_rows, ADAPTER_RANK).astype(jnp.float32)[:, None], (low_rows, LANES)
    )
    notes = jnp.concatenate([own_routes.T.astype(jnp.float32), own_gates.T, wanted], axis=0)

    across = [(i, i ^ 2) for i in range(tp_count)]
    beside = [(i, i ^ 1) for i in range(tp_count)]

    gate_far, up_far, down_far = (
        lax.ppermute(piece, "tp", across)
        for piece in (expert_gate_weight, expert_up_weight, expert_down_weight)
    )

    def quarters(piece, far):
        near = lax.ppermute(piece, "tp", beside)
        return [piece, far, near, lax.ppermute(far, "tp", beside)]

    stored = adapter_down_maps.shape[0]
    down_width = width // tp_count
    down_part = lax.dynamic_slice_in_dim(adapter_down_maps, tp_place * down_width, down_width, 2)
    table = jnp.concatenate([down_part, adapter_query_up, adapter_value_up], axis=2)
    adapter_width = table.shape[2]
    table = table.reshape(stored * ADAPTER_RANK, adapter_width)
    in_vmem = pl.BlockSpec(memory_space=pltpu.VMEM)
    in_place = pl.BlockSpec(memory_space=pl.ANY)
    dma = pltpu.SemaphoreType.DMA
    bf16 = jnp.bfloat16
    group_x, notes, down_selected, query_up_selected, value_up_selected = pl.pallas_call(
        functools.partial(opening_kernel, req_count, tp_count, stored),
        in_specs=[in_vmem] * 3,
        out_specs=[in_place] + [in_vmem] * 4,
        out_shape=[
            jax.ShapeDtypeStruct((tp_count, own_rows, width), bf16),
            jax.ShapeDtypeStruct((req_count, 2 * TOP, own_rows), jnp.float32),
            jax.ShapeDtypeStruct((low_rows, width), bf16),
            jax.ShapeDtypeStruct((low_rows, query_width), bf16),
            jax.ShapeDtypeStruct((low_rows, kv_width), bf16),
        ],
        scratch_shapes=[
            pltpu.VMEM((req_count,) + notes.shape, jnp.float32),
            pltpu.VMEM((req_count, low_rows, adapter_width), bf16),
            pltpu.VMEM((req_count, low_rows, adapter_width), bf16),
            pltpu.VMEM((low_rows, down_width), bf16),
            pltpu.VMEM((tp_count, low_rows, down_width), bf16),
            dma, dma((3,)), dma((3,)), dma((req_count,)), dma((req_count,)),
            dma((req_count,)), dma((req_count,)), dma((tp_count,)), dma((tp_count,)),
        ],
        compiler_params=pltpu.CompilerParams(
            collective_id=1, has_side_effects=True, vmem_limit_bytes=32 << 20
        ),
        cost_estimate=pl.CostEstimate(
            flops=0, bytes_accessed=90_000_000, transcendentals=0
        ),
        name="opening",
    )(tokens, notes, table)
    group_x = group_x.reshape(group_size, width)
    all_routes = notes[:, :TOP].astype(jnp.int32)
    all_gates = notes[:, TOP:]

    new_labels = token_request[0]
    old_labels = cached_request[0]
    labels = jnp.arange(GROUP_REQUESTS, dtype=jnp.int32)
    member = new_labels[:, None] == labels[None, :]
    old_below = jnp.sum((old_labels[:, None] < labels[None, :]).astype(jnp.int32), axis=0)
    old_upto = jnp.sum((old_labels[:, None] <= labels[None, :]).astype(jnp.int32), axis=0)
    new_below = jnp.sum((new_labels[:, None] < labels[None, :]).astype(jnp.int32), axis=0)

    def by_token(table):
        return jnp.sum(jnp.where(member, table[None, :], 0), axis=1)

    place = jnp.arange(group_size, dtype=jnp.int32)
    old_start, old_end, new_start = by_token(old_below), by_token(old_upto), by_token(new_below)
    positions = place - new_start + old_end - old_start
    bounds = jnp.stack([old_start, old_end, new_start, place + 1] * 2, axis=0)
    block_start = jnp.min(old_start.reshape(-1, QUERY_BLOCK), axis=1)
    block_end = jnp.max(old_end.reshape(-1, QUERY_BLOCK), axis=1)
    block_range = jnp.stack(
        [block_start // KEY_BLOCK, (block_end + KEY_BLOCK - 1) // KEY_BLOCK], axis=0
    )
    spread = jnp.repeat(member.astype(jnp.float32), ADAPTER_RANK, axis=1)
    half = HEAD_SIZE // 2
    lane = jnp.arange(LANES, dtype=jnp.int32)
    inverse_freq = rope_theta ** (-((lane % half).astype(jnp.float32) / half))
    angles = positions.astype(jnp.float32)[:, None] * inverse_freq[None, :]
    cosine = jnp.cos(angles)
    sine = jnp.sin(angles) * jnp.where(lane % HEAD_SIZE < half, -1.0, 1.0)[None, :]

    whole = lambda shape: pl.BlockSpec(shape, lambda i, *_: (0,) * len(shape))
    by_row = lambda rows, columns: pl.BlockSpec((rows, columns), lambda i, *_: (i, 0))
    rows = 2 * QUERY_BLOCK
    queries, fresh_keys, fresh_values = pl.pallas_call(
        functools.partial(projection_kernel, heads, kv_heads),
        grid=(group_size // rows,),
        in_specs=[
            by_row(rows, width), whole((1, width)), whole((width, query_width)),
            whole((width, kv_width)), whole((width, kv_width)), whole((low_rows, width)),
            whole((low_rows, query_width)), whole((low_rows, kv_width)), by_row(rows, low_rows),
            by_row(rows, LANES), by_row(rows, LANES),
        ],
        out_specs=[
            pl.BlockSpec((heads, rows, LANES), lambda i: (0, i, 0)),
            by_row(rows, kv_width), by_row(rows, kv_width),
        ],
        out_shape=[
            jax.ShapeDtypeStruct((heads, group_size, LANES), jnp.bfloat16),
            jax.ShapeDtypeStruct((group_size, kv_width), jnp.bfloat16),
            jax.ShapeDtypeStruct((group_size, kv_width), jnp.bfloat16),
        ],
        cost_estimate=pl.CostEstimate(
            flops=2 * group_size * width * (query_width + 2 * kv_width + low_rows),
            bytes_accessed=6_000_000, transcendentals=0,
        ),
        name="projections",
    )(
        group_x, attention_norm_gain[None, :], query_projection, key_projection, value_projection,
        down_selected, query_up_selected, value_up_selected, spread, cosine, sine,
    )

    context = cached_keys.shape[0]
    partial_rows = pl.pallas_call(
        functools.partial(attention_kernel, heads, kv_heads),
        grid_spec=pltpu.PrefetchScalarGridSpec(
            num_scalar_prefetch=1,
            grid=(group_size // QUERY_BLOCK,),
            in_specs=[
                pl.BlockSpec((heads, QUERY_BLOCK, LANES), lambda i, *_: (0, i, 0)),
                whole((context, kv_width)), whole((context, kv_width)),
                whole((group_size, kv_width)), whole((group_size, kv_width)),
                pl.BlockSpec((8, QUERY_BLOCK), lambda i, *_: (0, i)),
                whole((query_width, width)),
            ],
            out_specs=by_row(QUERY_BLOCK, width),
        ),
        out_shape=jax.ShapeDtypeStruct((group_size, width), jnp.bfloat16),
        compiler_params=pltpu.CompilerParams(vmem_limit_bytes=40 << 20),
        cost_estimate=pl.CostEstimate(
            flops=10_000_000_000, bytes_accessed=6_000_000, transcendentals=14_000_000
        ),
        name="attention",
    )(
        block_range, queries, cached_keys, cached_values, fresh_keys, fresh_values, bounds,
        attention_output_weight,
    )
    partial_rows, gate_far = lax.optimization_barrier((partial_rows, gate_far))
    gates = quarters(expert_gate_weight, gate_far)
    line = req_count // 2
    resid_own, arrived = pl.pallas_call(
        functools.partial(middle_kernel, req_count, tp_count),
        in_specs=[in_vmem] * 3,
        out_specs=[in_vmem, in_place],
        out_shape=[
            jax.ShapeDtypeStruct((own_rows, width), bf16),
            jax.ShapeDtypeStruct((req_count, own_rows, width), bf16),
        ],
        scratch_shapes=[
            pltpu.VMEM((2, own_rows, width), bf16), pltpu.VMEM((own_rows, width), bf16),
            pltpu.VMEM((own_rows, width), bf16), pltpu.VMEM((own_rows, width), bf16),
            dma, dma((3,)), dma((3,)), dma((line,)), dma((line,)), dma((line,)), dma((line,)),
        ],
        compiler_params=pltpu.CompilerParams(
            collective_id=2, has_side_effects=True, vmem_limit_bytes=32 << 20
        ),
        cost_estimate=pl.CostEstimate(
            flops=0, bytes_accessed=200_000_000, transcendentals=0
        ),
        name="middle",
    )(partial_rows.reshape(tp_count, own_rows, width), tokens, expert_norm_gain[None, :])
    arrived = arrived.reshape(req_count * own_rows, width)
    arrived, up_far, down_far = lax.optimization_barrier((arrived, up_far, down_far))
    ups = quarters(expert_up_weight, up_far)
    downs = quarters(expert_down_weight, down_far)

    local_experts = expert_gate_weight.shape[0]
    total_rows = req_count * own_rows
    chunk_rows = min(8, req_count) * own_rows
    chunk_blocks = chunk_rows // own_rows
    slots = chunk_blocks * capacity
    expert_ids = req_place * local_experts + jnp.arange(local_experts, dtype=jnp.int32)
    hits = all_routes[None] == expert_ids[:, None, None, None]
    expert_weight = jnp.sum(jnp.where(hits, all_gates[None], 0.0), axis=2)
    named = jnp.any(hits, axis=2)
    earlier = jnp.arange(own_rows)[:, None] < jnp.arange(own_rows)[None, :]
    rank = jnp.einsum(
        "ebt,tu->ebu", named.astype(jnp.bfloat16), earlier.astype(jnp.bfloat16),
        preferred_element_type=jnp.float32,
    ).astype(jnp.int32)
    block_base = (jnp.arange(req_count, dtype=jnp.int32) % chunk_blocks) * capacity
    slot_of = jnp.where(named, rank + block_base[None, :, None], -1)
    slot_of = slot_of.reshape(local_experts, 1, total_rows)
    expert_weight = expert_weight.reshape(local_experts, 1, total_rows)

    quarter = expert_gate_weight.shape[2]
    row_spec = pl.BlockSpec((1, 1, chunk_rows), lambda c, e: (e, 0, c))
    moe = pl.pallas_call(
        functools.partial(expert_kernel, slots),
        grid=(total_rows // chunk_rows, local_experts),
        in_specs=[pl.BlockSpec((chunk_rows, width), lambda c, e: (c, 0)), row_spec, row_spec]
        + [pl.BlockSpec((1, width, quarter), lambda c, e: (e, 0, 0))] * 8
        + [pl.BlockSpec((1, quarter, width), lambda c, e: (e, 0, 0))] * 4,
        out_specs=pl.BlockSpec((chunk_rows, width), lambda c, e: (c, 0)),
        out_shape=jax.ShapeDtypeStruct((total_rows, width), jnp.bfloat16),
        scratch_shapes=[pltpu.VMEM((chunk_rows, width), jnp.float32)],
        compiler_params=pltpu.CompilerParams(vmem_limit_bytes=52 << 20),
        cost_estimate=pl.CostEstimate(
            flops=12_000_000_000, bytes_accessed=26_000_000, transcendentals=600_000
        ),
        name="experts",
    )(arrived, slot_of, expert_weight, *gates, *ups, *downs)
    return pl.pallas_call(
        functools.partial(closing_kernel, req_count),
        in_specs=[in_vmem] * 2,
        out_specs=in_vmem,
        out_shape=jax.ShapeDtypeStruct((own_rows, width), bf16),
        scratch_shapes=[pltpu.VMEM((line, own_rows, width), bf16)] * 3
        + [dma((line,))] * 4,
        compiler_params=pltpu.CompilerParams(
            collective_id=3, has_side_effects=True, vmem_limit_bytes=48 << 20
        ),
        cost_estimate=pl.CostEstimate(
            flops=0, bytes_accessed=150_000_000, transcendentals=0
        ),
        name="closing",
    )(moe.reshape(req_count, own_rows, width), resid_own)


def solution(mesh):
    return jax.shard_map(
        on_device,
        mesh=mesh,
        in_specs=(
            P(("req", "tp"), None),
            P(),
            P(),
            P(None, "tp"),
            P(None, "tp"),
            P(None, "tp"),
            P("tp", None),
            P("req", "tp"),
            P("req", "tp"),
            P("req", None),
            P("req", None),
            P("req", None),
            P(),
            P("req", None, None),
            P("req", None, "tp"),
            P("req", None, "tp"),
            P("req", None),
            P("req", None),
            P("req", None, "tp"),
            P("req", None, "tp"),
            P("req", "tp", None),
        ),
        out_specs=P(("req", "tp"), None),
        check_vma=False,
    )
```

```python
import functools

import jax
import jax.numpy as jnp
from jax import lax
from jax.experimental import pallas as pl
from jax.experimental.pallas import tpu as pltpu
from jax.sharding import PartitionSpec as P

HEAD_SIZE = 64
EXPERTS = 32
TOP = 8
ADAPTER_RANK = 16
GROUP_REQUESTS = 4
LANES = 128
KEY_BLOCK = 512
QUERY_BLOCK = 128
HIDDEN_SCORE = -1e30

norm_eps = 1e-05
rope_theta = 10000.0


def rms_norm(row_block, gain_row):
    values = row_block.astype(jnp.float32)
    inv_rms = lax.rsqrt(jnp.mean(values * values, axis=-1, keepdims=True) + norm_eps)
    return (values * inv_rms * gain_row.astype(jnp.float32)).astype(jnp.bfloat16)


def dot_f32(left, right):
    return jnp.dot(left, right, preferred_element_type=jnp.float32)


def projection_kernel(
    heads, kv_heads, x_ref, gain_ref, wq_ref, wk_ref, wv_ref, down_ref, qup_ref, vup_ref,
    spread_ref, cos_ref, sin_ref, q_ref, k_ref, v_ref
):
    normed = rms_norm(x_ref[...], gain_ref[...])
    low = lax.dot_general(
        normed, down_ref[...], (((1,), (1,)), ((), ())), preferred_element_type=jnp.float32
    )
    low = (low * spread_ref[...]).astype(jnp.bfloat16)
    q = dot_f32(normed, wq_ref[...]) + dot_f32(low, qup_ref[...])
    k = dot_f32(normed, wk_ref[...])
    v_ref[...] = (dot_f32(normed, wv_ref[...]) + dot_f32(low, vup_ref[...])).astype(jnp.bfloat16)
    cosine, sine = cos_ref[...], sin_ref[...]
    lane = lax.broadcasted_iota(jnp.int32, cosine.shape, 1)
    front = lane % HEAD_SIZE < HEAD_SIZE // 2
    upper = lane >= HEAD_SIZE

    def turn(piece):
        partner = jnp.where(
            front,
            pltpu.roll(piece, LANES - HEAD_SIZE // 2, 1),
            pltpu.roll(piece, HEAD_SIZE // 2, 1),
        )
        return piece * cosine + partner * sine

    k_ref[...] = turn(k).astype(jnp.bfloat16)
    per_kv = heads // kv_heads
    for piece_id in range(heads // 2):
        turned = turn(q[:, piece_id * LANES : (piece_id + 1) * LANES]) * HEAD_SIZE ** (-0.5)
        swapped = pltpu.roll(turned, HEAD_SIZE, 1)
        for side in range(2):
            head = 2 * piece_id + side
            kv = head // per_kv
            source = turned if kv == side else swapped
            keep = upper if kv == 1 else jnp.logical_not(upper)
            q_ref[head] = jnp.where(keep, source, 0.0).astype(jnp.bfloat16)


def attention_kernel(
    heads, kv_heads, range_ref, q_ref, ck_ref, cv_ref, nk_ref, nv_ref, bound_ref, wo_ref, out_ref
):
    block = pl.program_id(0)
    rows = q_ref.shape[1]
    queries = q_ref[...].reshape(heads * rows, LANES)
    bounds = jnp.concatenate([bound_ref[...]] * heads, axis=1)
    old_start, old_end, new_start, new_end = (bounds[i : i + 1] for i in range(4))

    def score(keys, first, start, end):
        values = lax.dot_general(
            keys, queries, (((1,), (1,)), ((), ())), preferred_element_type=jnp.float32
        )
        place = lax.broadcasted_iota(jnp.int32, values.shape, 0) + first
        return jnp.where((place >= start) & (place < end), values, HIDDEN_SCORE)

    def gather(weights, values):
        return lax.dot_general(
            values, weights.astype(jnp.bfloat16), (((0,), (0,)), ((), ())),
            preferred_element_type=jnp.float32,
        )

    scores = score(nk_ref[...], 0, new_start, new_end)
    top = jnp.max(scores, axis=0, keepdims=True)
    weights = jnp.exp(scores - top)
    total = jnp.sum(weights, axis=0, keepdims=True)
    mixed = gather(weights, nv_ref[...])

    def step(index, carry):
        top, total, mixed = carry
        first = pl.multiple_of(index * KEY_BLOCK, KEY_BLOCK)
        scores = score(ck_ref[pl.ds(first, KEY_BLOCK), :], first, old_start, old_end)
        new_top = jnp.maximum(top, jnp.max(scores, axis=0, keepdims=True))
        shrink = jnp.exp(top - new_top)
        weights = jnp.exp(scores - new_top)
        total = total * shrink + jnp.sum(weights, axis=0, keepdims=True)
        mixed = mixed * shrink + gather(weights, cv_ref[pl.ds(first, KEY_BLOCK), :])
        return new_top, total, mixed

    top, total, mixed = lax.fori_loop(
        range_ref[0, block], range_ref[1, block], step, (top, total, mixed)
    )
    mixed = mixed / total
    per_kv = heads // kv_heads
    pieces = []
    for piece_id in range(heads // 2):
        halves = []
        for head in (2 * piece_id, 2 * piece_id + 1):
            kv = head // per_kv
            halves.append(
                mixed[kv * HEAD_SIZE : (kv + 1) * HEAD_SIZE, head * rows : (head + 1) * rows]
            )
        pieces.append(jnp.transpose(jnp.concatenate(halves, axis=0)).astype(jnp.bfloat16))
    out_ref[...] = dot_f32(jnp.concatenate(pieces, axis=1), wo_ref[...]).astype(jnp.bfloat16)


def expert_kernel(slots, x_ref, slot_ref, weight_ref, *refs):
    gates, ups, downs = refs[0:4], refs[4:8], refs[8:12]
    out_ref, total_ref = refs[12:]
    expert = pl.program_id(1)
    rows = x_ref.shape[0]
    chosen = lax.broadcasted_iota(jnp.int32, (slots, rows), 0) == slot_ref[0]
    row_weight = jnp.sum(jnp.where(chosen, weight_ref[0], 0.0), axis=1, keepdims=True)
    pick = jnp.where(chosen, 1.0, 0.0).astype(jnp.bfloat16)
    picked = dot_f32(pick, x_ref[...]).astype(jnp.bfloat16)
    gate = dot_f32(picked, jnp.concatenate([ref[0] for ref in gates], axis=1))
    up = dot_f32(picked, jnp.concatenate([ref[0] for ref in ups], axis=1))
    hidden = (jax.nn.silu(gate) * up).astype(jnp.bfloat16)
    result = dot_f32(hidden, jnp.concatenate([ref[0] for ref in downs], axis=0))
    result = (result * row_weight).astype(jnp.bfloat16)
    spread = lax.dot_general(
        pick, result, (((0,), (0,)), ((), ())), preferred_element_type=jnp.float32
    )

    @pl.when(expert == 0)
    def _():
        total_ref[...] = spread

    @pl.when(expert > 0)
    def _():
        total_ref[...] += spread

    @pl.when(expert == pl.num_programs(1) - 1)
    def _():
        out_ref[...] = total_ref[...].astype(jnp.bfloat16)


MESH = pl.DeviceIdType.MESH


def send_to(source, target, send_sem, recv_sem, axis, device):
    return pltpu.make_async_remote_copy(
        src_ref=source, dst_ref=target, send_sem=send_sem, recv_sem=recv_sem,
        device_id={axis: device}, device_id_type=MESH,
    )


def greet(peers):
    barrier = pltpu.get_barrier_semaphore()
    for axis, device in peers:
        pl.semaphore_signal(barrier, inc=1, device_id={axis: device}, device_id_type=MESH)
    pl.semaphore_wait(barrier, len(peers))


def core_partner(place):
    return place + 1 - 2 * (place % 2)


def token_kernel(tp_count, tokens_ref, group_ref, local_sem, x_send, x_recv):
    here = lax.axis_index("tp")
    beside, across = core_partner(here), (here + 2) % tp_count
    greet([("tp", beside), ("tp", across)])
    to_across = send_to(tokens_ref, group_ref.at[here], x_send.at[0], x_recv.at[0], "tp", across)
    to_across.start()
    to_beside = send_to(tokens_ref, group_ref.at[here], x_send.at[1], x_recv.at[1], "tp", beside)
    to_beside.start()
    own_copy = pltpu.make_async_copy(tokens_ref, group_ref.at[here], local_sem)
    own_copy.start()
    to_across.wait()
    forward = send_to(group_ref.at[across], group_ref.at[across], x_send.at[2], x_recv.at[2], "tp",
                      beside)
    forward.start()
    own_copy.wait()
    to_beside.wait()
    forward.wait()


def opening_kernel(
    req_count, stored, notes_ref, table_ref, all_notes_ref, down_ref, qup_ref, vup_ref,
    noted, chosen, arrived, downs, n_send, n_recv, a_send, a_recv, d_send, d_recv
):
    me, here = lax.axis_index("req"), lax.axis_index("tp")
    beside = core_partner(here)
    greet([("req", (me + step) % req_count) for step in range(1, req_count)] + [("tp", beside)])
    note_copies = []
    for step in range(1, req_count):
        copy = send_to(notes_ref, noted.at[step], n_send.at[step], n_recv.at[step], "req",
                       (me + step) % req_count)
        copy.start()
        note_copies.append(copy)

    rows = GROUP_REQUESTS * ADAPTER_RANK
    depth = stored * ADAPTER_RANK
    lane = lax.broadcasted_iota(jnp.int32, (rows, depth), 1)
    row = lax.broadcasted_iota(jnp.int32, (rows, depth), 0)
    same_rank = lane % ADAPTER_RANK == row % ADAPTER_RANK
    slot = (me * stored + lane // ADAPTER_RANK).astype(jnp.float32)

    def select(notes):
        wanted = notes[2 * TOP :, :depth]
        pick = jnp.where(same_rank & (wanted == slot), 1.0, 0.0).astype(jnp.bfloat16)
        return dot_f32(pick, table_ref[...])

    total = select(notes_ref[...])
    all_notes_ref[me] = notes_ref[: 2 * TOP, :]
    adapter_copies = []
    for step in range(1, req_count):
        note_copies[step - 1].wait()
        notes = noted[step]
        source = (me + req_count - step) % req_count
        all_notes_ref[source] = notes[: 2 * TOP, :]
        chosen[step] = select(notes).astype(jnp.bfloat16)
        copy = send_to(chosen.at[step], arrived.at[step], a_send.at[step], a_recv.at[step], "req",
                       source)
        copy.start()
        adapter_copies.append(copy)
    for step in range(1, req_count):
        adapter_copies[step - 1].wait()
        total = total + arrived[step].astype(jnp.float32)
    total = total.astype(jnp.bfloat16)
    down_width = downs.shape[2]
    query_width = qup_ref.shape[1]
    core = here % 2
    downs[core] = total[:, :down_width]
    copy = send_to(downs.at[core], downs.at[core], d_send, d_recv, "tp", beside)
    copy.start()
    qup_ref[...] = total[:, down_width : down_width + query_width]
    vup_ref[...] = total[:, down_width + query_width :]
    copy.wait()
    down_ref[...] = jnp.concatenate([downs[0], downs[1]], axis=1)


def middle_kernel(
    req_count, tp_count, partial_ref, tokens_ref, gain_ref, weight_ref,
    resid_ref, arrived_ref, weight_far_ref, weight_near_ref, weight_far_near_ref,
    pair, joined, far, ffn, local_sem, p_send, p_recv, z_send, z_recv, f_send, f_recv,
    n_send, n_recv, w_send, w_recv, v_send, v_recv
):
    me, here = lax.axis_index("req"), lax.axis_index("tp")
    beside, across = core_partner(here), (here + 2) % tp_count
    partner = core_partner(me)
    line = req_count // 2
    greet(
        [("tp", beside), ("tp", across), ("req", partner)]
        + [("req", (me + 2 * step) % req_count) for step in range(1, line)]
    )
    f32 = jnp.float32
    second = send_to(partial_ref.at[(beside + 2) % tp_count], pair.at[1], p_send.at[1],
                     p_recv.at[1], "tp", beside)
    second.start()
    first = send_to(partial_ref.at[beside], pair.at[0], p_send.at[0], p_recv.at[0], "tp", beside)
    first.start()
    second.wait()
    joined[...] = (partial_ref[across].astype(f32) + pair[1].astype(f32)).astype(jnp.bfloat16)
    last = send_to(joined, far, p_send.at[2], p_recv.at[2], "tp", across)
    last.start()
    pieces = weight_ref.shape[0]
    far_copies = []
    for piece in range(pieces):
        copy = send_to(weight_ref.at[piece], weight_far_ref.at[piece], w_send.at[piece],
                       w_recv.at[piece], "tp", across)
        copy.start()
        far_copies.append(copy)
    first.wait()
    near_copy = send_to(weight_ref, weight_near_ref, n_send, n_recv, "tp", beside)
    near_copy.start()
    own = partial_ref[here].astype(f32) + pair[0].astype(f32) + tokens_ref[...].astype(f32)
    last.wait()
    resid = (own + far[...].astype(f32)).astype(jnp.bfloat16)
    resid_ref[...] = resid
    ffn[...] = rms_norm(resid, gain_ref[...])
    line_copies = []
    for step in range(1, line):
        copy = send_to(ffn, arrived_ref.at[me], z_send.at[step], z_recv.at[step], "req",
                       (me + 2 * step) % req_count)
        copy.start()
        line_copies.append(copy)
    to_partner = send_to(ffn, arrived_ref.at[me], f_send.at[0], f_recv.at[0], "req", partner)
    to_partner.start()
    own_copy = pltpu.make_async_copy(ffn, arrived_ref.at[me], local_sem)
    own_copy.start()
    forwards = []
    for step in range(1, line):
        line_copies[step - 1].wait()
        source = (me + req_count - 2 * step) % req_count
        copy = send_to(arrived_ref.at[source], arrived_ref.at[source], f_send.at[step],
                       f_recv.at[step], "req", partner)
        copy.start()
        forwards.append(copy)
    near_forwards = []
    for piece in range(pieces):
        far_copies[piece].wait()
        copy = send_to(weight_far_ref.at[piece], weight_far_near_ref.at[piece], v_send.at[piece],
                       v_recv.at[piece], "tp", beside)
        copy.start()
        near_forwards.append(copy)
    own_copy.wait()
    to_partner.wait()
    near_copy.wait()
    for copy in forwards + near_forwards:
        copy.wait()


def closing_kernel(
    req_count, moe_ref, resid_ref, out_ref, beside_in, line_out, line_in,
    y_send, y_recv, z_send, z_recv
):
    me = lax.axis_index("req")
    partner = core_partner(me)
    line = req_count // 2
    greet(
        [("req", partner)]
        + [("req", (me + 2 * step) % req_count) for step in range(1, line)]
    )
    f32 = jnp.float32
    order = list(range(1, line)) + [0]
    beside_copies = {}
    for step in order:
        copy = send_to(moe_ref.at[(partner + 2 * step) % req_count], beside_in.at[step],
                       y_send.at[step], y_recv.at[step], "req", partner)
        copy.start()
        beside_copies[step] = copy
    line_copies = []
    for step in range(1, line):
        target = (me + 2 * step) % req_count
        beside_copies[step].wait()
        line_out[step] = (
            moe_ref[target].astype(f32) + beside_in[step].astype(f32)
        ).astype(jnp.bfloat16)
        copy = send_to(line_out.at[step], line_in.at[step], z_send.at[step], z_recv.at[step],
                       "req", target)
        copy.start()
        line_copies.append(copy)
    beside_copies[0].wait()
    total = resid_ref[...].astype(f32) + moe_ref[me].astype(f32) + beside_in[0].astype(f32)
    for step in range(1, line):
        line_copies[step - 1].wait()
        total = total + line_in[step].astype(f32)
    out_ref[...] = total.astype(jnp.bfloat16)


def on_device(
    tokens,
    attention_norm_gain,
    expert_norm_gain,
    query_projection,
    key_projection,
    value_projection,
    attention_output_weight,
    cached_keys,
    cached_values,
    token_request,
    cached_request,
    adapter_of_request,
    adapter_table_row,
    adapter_down_maps,
    adapter_query_up,
    adapter_value_up,
    routes,
    routed_weight,
    expert_gate_weight,
    expert_up_weight,
    expert_down_weight,
):
    tp_count = lax.axis_size("tp")
    tp_place = lax.axis_index("tp")
    req_count = lax.axis_size("req")
    req_place = lax.axis_index("req")
    own_rows, width = tokens.shape
    group_size = own_rows * tp_count
    query_width = query_projection.shape[1]
    kv_width = key_projection.shape[1]
    heads = query_width // HEAD_SIZE
    kv_heads = kv_width // HEAD_SIZE
    low_rows = GROUP_REQUESTS * ADAPTER_RANK
    assert tp_count == 4 and kv_heads == 2 and own_rows == QUERY_BLOCK
    capacity = own_rows * TOP // EXPERTS + 2

    own_routes = lax.dynamic_slice_in_dim(routes, tp_place * own_rows, own_rows, 0)
    own_gates = lax.dynamic_slice_in_dim(routed_weight, tp_place * own_rows, own_rows, 0)
    catalog = jnp.arange(adapter_table_row.shape[0], dtype=jnp.int32)
    table_rows = jnp.sum(
        (adapter_of_request[0][:, None] == catalog[None, :]).astype(jnp.int32)
        * adapter_table_row[None, :],
        axis=1,
    )
    wanted = jnp.broadcast_to(
        jnp.repeat(table_rows, ADAPTER_RANK).astype(jnp.float32)[:, None], (low_rows, LANES)
    )
    notes = jnp.concatenate([own_routes.T.astype(jnp.float32), own_gates.T, wanted], axis=0)

    in_vmem = pl.BlockSpec(memory_space=pltpu.VMEM)
    in_place = pl.BlockSpec(memory_space=pl.ANY)
    dma = pltpu.SemaphoreType.DMA
    bf16 = jnp.bfloat16
    group_x = pl.pallas_call(
        functools.partial(token_kernel, tp_count),
        in_specs=[in_vmem],
        out_specs=in_place,
        out_shape=jax.ShapeDtypeStruct((tp_count, own_rows, width), bf16),
        scratch_shapes=[dma, dma((3,)), dma((3,))],
        compiler_params=pltpu.CompilerParams(
            collective_id=4, has_side_effects=True, vmem_limit_bytes=8 << 20
        ),
        cost_estimate=pl.CostEstimate(flops=0, bytes_accessed=40_000_000, transcendentals=0),
        name="tokens",
    )(tokens)
    group_x, expert_gate_weight, expert_up_weight = lax.optimization_barrier(
        (group_x, expert_gate_weight, expert_up_weight)
    )

    across = [(i, i ^ 2) for i in range(tp_count)]
    beside = [(i, i ^ 1) for i in range(tp_count)]

    gate_far, up_far = (
        lax.ppermute(piece, "tp", across) for piece in (expert_gate_weight, expert_up_weight)
    )

    def quarters(piece, far):
        near = lax.ppermute(piece, "tp", beside)
        return [piece, far, near, lax.ppermute(far, "tp", beside)]

    stored = adapter_down_maps.shape[0]
    down_width = width // 2
    down_part = lax.dynamic_slice_in_dim(
        adapter_down_maps, tp_place % 2 * down_width, down_width, 2
    )
    table = jnp.concatenate([down_part, adapter_query_up, adapter_value_up], axis=2)
    adapter_width = table.shape[2]
    table = table.reshape(stored * ADAPTER_RANK, adapter_width)
    notes, group_x = lax.optimization_barrier((notes, group_x))
    notes, down_selected, query_up_selected, value_up_selected = pl.pallas_call(
        functools.partial(opening_kernel, req_count, stored),
        in_specs=[in_vmem] * 2,
        out_specs=[in_vmem] * 4,
        out_shape=[
            jax.ShapeDtypeStruct((req_count, 2 * TOP, own_rows), jnp.float32),
            jax.ShapeDtypeStruct((low_rows, width), bf16),
            jax.ShapeDtypeStruct((low_rows, query_width), bf16),
            jax.ShapeDtypeStruct((low_rows, kv_width), bf16),
        ],
        scratch_shapes=[
            pltpu.VMEM((req_count,) + notes.shape, jnp.float32),
            pltpu.VMEM((req_count, low_rows, adapter_width), bf16),
            pltpu.VMEM((req_count, low_rows, adapter_width), bf16),
            pltpu.VMEM((2, low_rows, down_width), bf16),
            dma((req_count,)), dma((req_count,)), dma((req_count,)), dma((req_count,)), dma, dma,
        ],
        compiler_params=pltpu.CompilerParams(
            collective_id=1, has_side_effects=True, vmem_limit_bytes=32 << 20
        ),
        cost_estimate=pl.CostEstimate(flops=0, bytes_accessed=90_000_000, transcendentals=0),
        name="opening",
    )(notes, table)
    group_x = group_x.reshape(group_size, width)
    all_routes = notes[:, :TOP].astype(jnp.int32)
    all_gates = notes[:, TOP:]

    new_labels = token_request[0]
    old_labels = cached_request[0]
    labels = jnp.arange(GROUP_REQUESTS, dtype=jnp.int32)
    member = new_labels[:, None] == labels[None, :]
    old_below = jnp.sum((old_labels[:, None] < labels[None, :]).astype(jnp.int32), axis=0)
    old_upto = jnp.sum((old_labels[:, None] <= labels[None, :]).astype(jnp.int32), axis=0)
    new_below = jnp.sum((new_labels[:, None] < labels[None, :]).astype(jnp.int32), axis=0)

    def by_token(table):
        return jnp.sum(jnp.where(member, table[None, :], 0), axis=1)

    place = jnp.arange(group_size, dtype=jnp.int32)
    old_start, old_end, new_start = by_token(old_below), by_token(old_upto), by_token(new_below)
    positions = place - new_start + old_end - old_start
    bounds = jnp.stack([old_start, old_end, new_start, place + 1] * 2, axis=0)
    block_start = jnp.min(old_start.reshape(-1, QUERY_BLOCK), axis=1)
    block_end = jnp.max(old_end.reshape(-1, QUERY_BLOCK), axis=1)
    block_range = jnp.stack(
        [block_start // KEY_BLOCK, (block_end + KEY_BLOCK - 1) // KEY_BLOCK], axis=0
    )
    spread = jnp.repeat(member.astype(jnp.float32), ADAPTER_RANK, axis=1)
    half = HEAD_SIZE // 2
    lane = jnp.arange(LANES, dtype=jnp.int32)
    inverse_freq = rope_theta ** (-((lane % half).astype(jnp.float32) / half))
    angles = positions.astype(jnp.float32)[:, None] * inverse_freq[None, :]
    cosine = jnp.cos(angles)
    sine = jnp.sin(angles) * jnp.where(lane % HEAD_SIZE < half, -1.0, 1.0)[None, :]

    whole = lambda shape: pl.BlockSpec(shape, lambda i, *_: (0,) * len(shape))
    by_row = lambda rows, columns: pl.BlockSpec((rows, columns), lambda i, *_: (i, 0))
    rows = 2 * QUERY_BLOCK
    queries, fresh_keys, fresh_values = pl.pallas_call(
        functools.partial(projection_kernel, heads, kv_heads),
        grid=(group_size // rows,),
        in_specs=[
            by_row(rows, width), whole((1, width)), whole((width, query_width)),
            whole((width, kv_width)), whole((width, kv_width)), whole((low_rows, width)),
            whole((low_rows, query_width)), whole((low_rows, kv_width)), by_row(rows, low_rows),
            by_row(rows, LANES), by_row(rows, LANES),
        ],
        out_specs=[
            pl.BlockSpec((heads, rows, LANES), lambda i: (0, i, 0)),
            by_row(rows, kv_width), by_row(rows, kv_width),
        ],
        out_shape=[
            jax.ShapeDtypeStruct((heads, group_size, LANES), jnp.bfloat16),
            jax.ShapeDtypeStruct((group_size, kv_width), jnp.bfloat16),
            jax.ShapeDtypeStruct((group_size, kv_width), jnp.bfloat16),
        ],
        cost_estimate=pl.CostEstimate(
            flops=2 * group_size * width * (query_width + 2 * kv_width + low_rows),
            bytes_accessed=6_000_000, transcendentals=0,
        ),
        name="projections",
    )(
        group_x, attention_norm_gain[None, :], query_projection, key_projection, value_projection,
        down_selected, query_up_selected, value_up_selected, spread, cosine, sine,
    )

    context = cached_keys.shape[0]
    partial_rows = pl.pallas_call(
        functools.partial(attention_kernel, heads, kv_heads),
        grid_spec=pltpu.PrefetchScalarGridSpec(
            num_scalar_prefetch=1,
            grid=(group_size // QUERY_BLOCK,),
            in_specs=[
                pl.BlockSpec((heads, QUERY_BLOCK, LANES), lambda i, *_: (0, i, 0)),
                whole((context, kv_width)), whole((context, kv_width)),
                whole((group_size, kv_width)), whole((group_size, kv_width)),
                pl.BlockSpec((8, QUERY_BLOCK), lambda i, *_: (0, i)),
                whole((query_width, width)),
            ],
            out_specs=by_row(QUERY_BLOCK, width),
        ),
        out_shape=jax.ShapeDtypeStruct((group_size, width), jnp.bfloat16),
        compiler_params=pltpu.CompilerParams(vmem_limit_bytes=40 << 20),
        cost_estimate=pl.CostEstimate(
            flops=10_000_000_000, bytes_accessed=6_000_000, transcendentals=14_000_000
        ),
        name="attention",
    )(
        block_range, queries, cached_keys, cached_values, fresh_keys, fresh_values, bounds,
        attention_output_weight,
    )
    partial_rows, gate_far = lax.optimization_barrier((partial_rows, gate_far))
    gates = quarters(expert_gate_weight, gate_far)
    line = req_count // 2
    weight_shape = jax.ShapeDtypeStruct(expert_down_weight.shape, bf16)
    pieces = expert_down_weight.shape[0]
    resid_own, arrived, down_far, down_near, down_far_near = pl.pallas_call(
        functools.partial(middle_kernel, req_count, tp_count),
        in_specs=[in_vmem] * 3 + [in_place],
        out_specs=[in_vmem] + [in_place] * 4,
        out_shape=[
            jax.ShapeDtypeStruct((own_rows, width), bf16),
            jax.ShapeDtypeStruct((req_count, own_rows, width), bf16),
            weight_shape, weight_shape, weight_shape,
        ],
        scratch_shapes=[
            pltpu.VMEM((2, own_rows, width), bf16), pltpu.VMEM((own_rows, width), bf16),
            pltpu.VMEM((own_rows, width), bf16), pltpu.VMEM((own_rows, width), bf16),
            dma, dma((3,)), dma((3,)), dma((line,)), dma((line,)), dma((line,)), dma((line,)),
            dma, dma, dma((pieces,)), dma((pieces,)), dma((pieces,)), dma((pieces,)),
        ],
        compiler_params=pltpu.CompilerParams(
            collective_id=2, has_side_effects=True, vmem_limit_bytes=32 << 20
        ),
        cost_estimate=pl.CostEstimate(
            flops=0, bytes_accessed=200_000_000, transcendentals=0
        ),
        name="middle",
    )(partial_rows.reshape(tp_count, own_rows, width), tokens, expert_norm_gain[None, :],
      expert_down_weight)
    arrived = arrived.reshape(req_count * own_rows, width)
    arrived, up_far = lax.optimization_barrier((arrived, up_far))
    ups = quarters(expert_up_weight, up_far)
    downs = [expert_down_weight, down_far, down_near, down_far_near]

    local_experts = expert_gate_weight.shape[0]
    total_rows = req_count * own_rows
    chunk_rows = min(8, req_count) * own_rows
    chunk_blocks = chunk_rows // own_rows
    slots = chunk_blocks * capacity
    expert_ids = req_place * local_experts + jnp.arange(local_experts, dtype=jnp.int32)
    hits = all_routes[None] == expert_ids[:, None, None, None]
    expert_weight = jnp.sum(jnp.where(hits, all_gates[None], 0.0), axis=2)
    named = jnp.any(hits, axis=2)
    earlier = jnp.arange(own_rows)[:, None] < jnp.arange(own_rows)[None, :]
    rank = jnp.einsum(
        "ebt,tu->ebu", named.astype(jnp.bfloat16), earlier.astype(jnp.bfloat16),
        preferred_element_type=jnp.float32,
    ).astype(jnp.int32)
    block_base = (jnp.arange(req_count, dtype=jnp.int32) % chunk_blocks) * capacity
    slot_of = jnp.where(named, rank + block_base[None, :, None], -1)
    slot_of = slot_of.reshape(local_experts, 1, total_rows)
    expert_weight = expert_weight.reshape(local_experts, 1, total_rows)

    quarter = expert_gate_weight.shape[2]
    row_spec = pl.BlockSpec((1, 1, chunk_rows), lambda c, e: (e, 0, c))
    moe = pl.pallas_call(
        functools.partial(expert_kernel, slots),
        grid=(total_rows // chunk_rows, local_experts),
        in_specs=[pl.BlockSpec((chunk_rows, width), lambda c, e: (c, 0)), row_spec, row_spec]
        + [pl.BlockSpec((1, width, quarter), lambda c, e: (e, 0, 0))] * 8
        + [pl.BlockSpec((1, quarter, width), lambda c, e: (e, 0, 0))] * 4,
        out_specs=pl.BlockSpec((chunk_rows, width), lambda c, e: (c, 0)),
        out_shape=jax.ShapeDtypeStruct((total_rows, width), jnp.bfloat16),
        scratch_shapes=[pltpu.VMEM((chunk_rows, width), jnp.float32)],
        compiler_params=pltpu.CompilerParams(vmem_limit_bytes=52 << 20),
        cost_estimate=pl.CostEstimate(
            flops=12_000_000_000, bytes_accessed=26_000_000, transcendentals=600_000
        ),
        name="experts",
    )(arrived, slot_of, expert_weight, *gates, *ups, *downs)
    return pl.pallas_call(
        functools.partial(closing_kernel, req_count),
        in_specs=[in_vmem] * 2,
        out_specs=in_vmem,
        out_shape=jax.ShapeDtypeStruct((own_rows, width), bf16),
        scratch_shapes=[pltpu.VMEM((line, own_rows, width), bf16)] * 3
        + [dma((line,))] * 4,
        compiler_params=pltpu.CompilerParams(
            collective_id=3, has_side_effects=True, vmem_limit_bytes=48 << 20
        ),
        cost_estimate=pl.CostEstimate(
            flops=0, bytes_accessed=150_000_000, transcendentals=0
        ),
        name="closing",
    )(moe.reshape(req_count, own_rows, width), resid_own)


def solution(mesh):
    return jax.shard_map(
        on_device,
        mesh=mesh,
        in_specs=(
            P(("req", "tp"), None),
            P(),
            P(),
            P(None, "tp"),
            P(None, "tp"),
            P(None, "tp"),
            P("tp", None),
            P("req", "tp"),
            P("req", "tp"),
            P("req", None),
            P("req", None),
            P("req", None),
            P(),
            P("req", None, None),
            P("req", None, "tp"),
            P("req", None, "tp"),
            P("req", None),
            P("req", None),
            P("req", None, "tp"),
            P("req", None, "tp"),
            P("req", "tp", None),
        ),
        out_specs=P(("req", "tp"), None),
        check_vma=False,
    )
```
